32 devices in a mesh: group: 16 (over z, y, core), mp: 2 (over x).
Axes of the slice: x: 2, y: 2, z: 4, core: 2. Of those that a mesh axis runs over, the one named last changes fastest.
Arguments:
- hidden: bfloat16 [8192, 2048], P('group'), may hold values from -12 to 12
- ln_gain: float32 [2048], replicated, may hold values from 0.5 to 1.5
- ln_shift: float32 [2048], replicated, may hold values from -2 to 2
- qkv_weight: bfloat16 [3, 2048, 1024], P(None, None, 'mp'), may hold values from -0.25 to 0.25
- qkv_bias: float32 [3, 1024], P(None, 'mp'), may hold values from -2 to 2
- out_weight: bfloat16 [1024, 2048], P('mp'), may hold values from -0.1875 to 0.1875
- up_weight: bfloat16 [2048, 4096], P(None, 'mp'), may hold values from -0.125 to 0.125
- up_bias: float32 [4096], P('mp'), may hold values from -3 to 3
- down_weight: bfloat16 [4096, 2048], P('mp'), may hold values from -0.09375 to 0.09375
- branch_bias: float32 [2048], replicated, may hold values from -2 to 2
- next_gain: float32 [2048], replicated, may hold values from 0.5 to 1.5
- next_shift: float32 [2048], replicated, may hold values from -2 to 2
- next_weight: bfloat16 [3, 2048, 1024], P(None, None, 'mp'), may hold values from -0.125 to 0.125
- next_bias: float32 [3, 1024], P(None, 'mp'), may hold values from -2 to 2
- key_cache: bfloat16 [128, 384, 1024], P('group', None, 'mp'), may hold values from -70 to 70
- value_cache: bfloat16 [128, 384, 1024], P('group', None, 'mp'), may hold values from -6 to 6
- tail_keys: bfloat16 [32, 2048, 1024], P('group', None, 'mp'), may hold values from -70 to 70
- tail_values: bfloat16 [32, 2048, 1024], P('group', None, 'mp'), may hold values from -6 to 6
- lengths: int32 [128], P('group'), may hold values from 1 to 384, as said below
- split_slot: int32 [32], P('group'), may hold values from 0 to 7, as said below
- tail_len: int32 [32], replicated, may hold values from 1 to 2048, as said below
- parents: int32 [8192], P('group'), may hold values from 0 to 63, as said below
- accepted: int32 [128, 8], P('group'), may hold values from 0 to 63, as said below
Outputs:
- new_hidden: bfloat16 [8192, 2048], P(('group', 'mp'))
- next_qkv: bfloat16 [3, 8192, 1024], P(None, 'group', 'mp')
- accepted_rows: bfloat16 [2, 1024, 1024], P(None, 'group', 'mp')
The draws below stay inside these ranges and needn't reach their ends.
Inputs may be any that keep to these rules, and one draw needn't show every extreme that they name: `lengths`: positions of each request in its own group; a request named in split_slot holds exactly 384. `split_slot`: distinct requests of the group, by index within the group; rank t continues at rank t of the group whose index differs in the lowest bit. `tail_len`: rank t of group g holds the continuation of the request named at rank t by split_slot of group g xor 1; some continuation holds exactly 2048. `parents`: each token's parent is an earlier token of its request; token 0 of each request names itself. `accepted`: distinct tokens of the request.
All inputs are finite; a program needn't handle non-finite values.
Results may differ from the reference program's by a relative error of at most 0.01.
Values may be sent and summed in bfloat16 or wider, within the bound.
No kernel may reach another device: no remote copies, remote signals or barrier semaphores. Data moves between devices by JAX's collectives and lax.ppermute only.
A program may use at most 192 MiB of HBM per device.

```python
import jax
import jax.numpy as jnp
from jax import lax

D = 2048
HEADS = 16
HD = 64
ROT = 32
FF = 4096
REQ = 8
DRAFT = 64
ACC = 8
CAP = 384
TCAP = 2048
TAILS = 2
REQS = 128
TOKENS = 8192
TAIL_ALL = 32
N_GROUP = 16
N_MP = 2


def split_grid(key):
    group_keys = jax.random.split(jax.random.fold_in(key, 11), N_GROUP)

    def choose(one_key):
        return jax.random.permutation(one_key, REQ)[:TAILS]
    return jax.vmap(choose)(group_keys).astype(jnp.int32)


def draw_split_slot(key, part):
    return split_grid(key).reshape(-1)


def draw_lengths(key, part):
    chosen = split_grid(key)
    marked = jnp.any(chosen[:, :, None] == jnp.arange(REQ, dtype=jnp.int32)[None, None, :], axis=1)
    base_len = jax.random.randint(jax.random.fold_in(key, 12), (N_GROUP, REQ), 1, CAP + 1)
    return jnp.where(marked, CAP, base_len).astype(jnp.int32).reshape(-1)


def draw_tail_len(key, part):
    base_len = jax.random.randint(jax.random.fold_in(key, 13), (N_GROUP * TAILS,), 1, TCAP + 1)
    fullest = jax.random.randint(jax.random.fold_in(key, 14), (), 0, N_GROUP * TAILS)
    filled = jnp.arange(N_GROUP * TAILS, dtype=jnp.int32) == fullest
    return jnp.where(filled, TCAP, base_len).astype(jnp.int32)


def draw_parents(key, part):
    limits = jnp.maximum(jnp.arange(DRAFT, dtype=jnp.int32), 1)
    picked = jax.random.randint(jax.random.fold_in(key, 15), (N_GROUP * REQ, DRAFT), 0, limits[None, :])
    return picked.astype(jnp.int32).reshape(-1)


def draw_accepted(key, part):
    row_keys = jax.random.split(jax.random.fold_in(key, 16), N_GROUP * REQ)

    def choose(one_key):
        return jax.random.permutation(one_key, DRAFT)[:ACC]
    return jax.vmap(choose)(row_keys).astype(jnp.int32)


def draw_hidden(key, part):
    key_a, key_b, key_c = jax.random.split(key, 3)
    noise = jax.random.normal(key_a, (TOKENS, D), jnp.float32)
    columns = jnp.exp(jax.random.uniform(key_b, (1, D), jnp.float32, jnp.log(0.3), jnp.log(3.0)))
    row_scale = jnp.exp(jax.random.uniform(key_c, (TOKENS, 1), jnp.float32, jnp.log(0.5), jnp.log(1.5)))
    return jnp.clip(noise * columns * row_scale, -12.0, 12.0).astype(jnp.bfloat16)


def key_rows(key, shape):
    key_a = jax.random.fold_in(key, 0)
    base_vals = jax.random.normal(key_a, shape, jnp.float32)
    return jnp.clip(base_vals, -70.0, 70.0)


def draw_key_cache(key, part):
    return key_rows(jax.random.fold_in(key, 21), (N_GROUP * REQ, CAP, HEADS * HD)).astype(jnp.bfloat16)


def draw_tail_keys(key, part):
    return key_rows(jax.random.fold_in(key, 22), (N_GROUP * TAILS, TCAP, HEADS * HD)).astype(jnp.bfloat16)


def levels(own_key, extent, shards, low, high):
    gain = 1.0
    for position, shards_of in shards:
        draws = jax.random.uniform(jax.random.fold_in(jax.random.fold_in(own_key, 6), position), (shards_of,), jnp.float32, low / len(shards), high / len(shards))
        gain = gain * jnp.repeat(jnp.exp(draws), extent[position] // shards_of).reshape((-1,) + (1,) * (len(extent) - 1 - position))
    return gain


def normal_values(rng, extent, width, reach, pieces=(), kind=jnp.bfloat16):
    result = jax.random.normal(rng, extent, jnp.float32) * width
    if len(pieces) > 0:
        result = levels(rng, extent, pieces, -0.22, 0.18) * result
    return jnp.clip(result, min=-reach, max=reach).astype(kind)


def setup_inputs(seed: int = 0) -> dict:
    key_of = jax.random.split(jax.random.key(seed), 24)
    hidden = draw_hidden(jax.random.fold_in(key_of[23], 71), 0)
    ln_gain = jnp.clip(1.0 + 0.1 * jax.random.normal(key_of[1], (D,), jnp.float32), 0.5, 1.5)
    ln_shift = normal_values(key_of[2], (D,), 0.3, 2.0, (), jnp.float32)
    qkv_weight = normal_values(key_of[3], (3, D, HEADS * HD), (D // 4) ** -0.5, 0.25, ((2, 2),))
    qkv_bias = normal_values(key_of[4], (3, HEADS * HD), 0.3, 2.0, ((1, 2),), jnp.float32)
    out_weight = normal_values(key_of[5], (HEADS * HD, D), (HEADS * HD) ** -0.5, 0.1875, ((0, 2),))
    up_weight = normal_values(key_of[6], (D, FF), D ** -0.5, 0.125, ((1, 2),))
    up_bias = normal_values(key_of[7], (FF,), 0.5, 3.0, ((0, 2),), jnp.float32)
    down_weight = normal_values(key_of[8], (FF, D), FF ** -0.5, 0.09375, ((0, 2),))
    branch_bias = normal_values(key_of[9], (D,), 0.3, 2.0, (), jnp.float32)
    next_gain = jnp.clip(1.0 + 0.1 * jax.random.normal(key_of[10], (D,), jnp.float32), 0.5, 1.5)
    next_shift = normal_values(key_of[11], (D,), 0.3, 2.0, (), jnp.float32)
    next_weight = normal_values(key_of[12], (3, D, HEADS * HD), D ** -0.5, 0.125, ((2, 2),))
    next_bias = normal_values(key_of[13], (3, HEADS * HD), 0.3, 2.0, ((1, 2),), jnp.float32)
    key_cache = draw_key_cache(jax.random.fold_in(key_of[23], 71), 0)
    value_cache = normal_values(key_of[15], (REQS, CAP, HEADS * HD), 1.0, 6.0, ((0, 16), (2, 2)))
    tail_keys = draw_tail_keys(jax.random.fold_in(key_of[23], 71), 0)
    tail_values = normal_values(key_of[17], (TAIL_ALL, TCAP, HEADS * HD), 1.0, 6.0, ((0, 16), (2, 2)))
    lengths = draw_lengths(jax.random.fold_in(key_of[23], 71), 0)
    split_slot = draw_split_slot(jax.random.fold_in(key_of[23], 71), 0)
    tail_len = draw_tail_len(jax.random.fold_in(key_of[23], 71), 0)
    parents = draw_parents(jax.random.fold_in(key_of[23], 71), 0)
    accepted = draw_accepted(jax.random.fold_in(key_of[23], 71), 0)
    return {"hidden": hidden, "ln_gain": ln_gain, "ln_shift": ln_shift, "qkv_weight": qkv_weight, "qkv_bias": qkv_bias, "out_weight": out_weight, "up_weight": up_weight, "up_bias": up_bias, "down_weight": down_weight, "branch_bias": branch_bias, "next_gain": next_gain, "next_shift": next_shift, "next_weight": next_weight, "next_bias": next_bias, "key_cache": key_cache, "value_cache": value_cache, "tail_keys": tail_keys, "tail_values": tail_values, "lengths": lengths, "split_slot": split_slot, "tail_len": tail_len, "parents": parents, "accepted": accepted}


epsilon = 1e-05
very_low = -1e+30
highest = lax.Precision.HIGHEST

def layer_norm(values_in, norm_gain, norm_bias):
    values_in = values_in.astype(jnp.float32)
    row_mean = lax.optimization_barrier(jnp.mean(values_in, axis=-1, keepdims=True))
    centred = values_in - row_mean
    variance = lax.optimization_barrier(jnp.mean(centred * centred, axis=-1, keepdims=True))
    return centred * lax.rsqrt(variance + epsilon) * norm_gain + norm_bias

def rotate(vectors, positions):
    half_rot = ROT // 2
    inverse = jnp.power(10000.0, -jnp.arange(half_rot, dtype=jnp.float32) * (2.0 / ROT))
    angles = positions[..., None] * inverse
    cosine = jnp.cos(angles)[..., None, :]
    sine_part = jnp.sin(angles)[..., None, :]
    leading = vectors[..., :half_rot]
    trailing = vectors[..., half_rot:ROT]
    return jnp.concatenate([leading * cosine - trailing * sine_part, trailing * cosine + leading * sine_part, vectors[..., ROT:]], axis=-1)

def ancestors(parent_ids):
    draft_ids = jnp.arange(DRAFT, dtype=jnp.int32)
    parent_hot = (parent_ids[:, :, None] == draft_ids[None, None, :]).astype(jnp.float32)
    ancestry = jnp.minimum(parent_hot + jnp.eye(DRAFT, dtype=jnp.float32)[None], 1.0)
    for squaring in range(DRAFT.bit_length()):
        ancestry = jnp.minimum(jnp.einsum('bij,bjk->bik', ancestry, ancestry, precision=highest), 1.0)
    return ancestry

def block_terms(queries, key_block, values, validity):
    scores = jnp.einsum('bqhe,bkhe->bhqk', queries.astype(jnp.float32), key_block.astype(jnp.float32)) * HD ** (-0.5)
    key_mask = validity[:, None]
    masked = jnp.where(key_mask, scores, very_low)
    row_peak = lax.optimization_barrier(jnp.max(masked, axis=-1))
    weights = jnp.where(key_mask, jnp.exp(masked - row_peak[..., None]), 0.0)
    weight_sum = lax.optimization_barrier(jnp.sum(weights, axis=-1))
    rounded = lax.optimization_barrier(weights.astype(jnp.bfloat16)).astype(jnp.float32)
    mixed_out = jnp.einsum('bhqk,bkhe->bhqe', rounded, values.astype(jnp.float32))
    return (mixed_out, row_peak, weight_sum)

def spread_tails(tail_part, split_hot):
    tail_mixed, tail_peak, tail_sum = tail_part
    has_tail = lax.optimization_barrier(jnp.sum(split_hot, axis=0))
    mixed_req = jnp.einsum('tr,thqe->rhqe', split_hot, tail_mixed, precision=highest)
    peak_req = jnp.where(has_tail[:, None, None] > 0.5, jnp.einsum('tr,thq->rhq', split_hot, tail_peak, precision=highest), very_low)
    sum_req = jnp.einsum('tr,thq->rhq', split_hot, tail_sum, precision=highest)
    return (mixed_req, peak_req, sum_req)

def combine(blocks):
    top_peak = blocks[0][1]
    for one_block in blocks[1:]:
        top_peak = jnp.maximum(top_peak, one_block[1])
    numerator = 0.0
    denominator = 0.0
    for one_block in blocks:
        factor = jnp.exp(one_block[1] - top_peak)
        numerator = numerator + factor[..., None] * one_block[0]
        denominator = denominator + factor * one_block[2]
    return numerator / denominator[..., None]

def reference(hidden, ln_gain, ln_shift, qkv_weight, qkv_bias, out_weight, up_weight, up_bias, down_weight, branch_bias, next_gain, next_shift, next_weight, next_bias, key_cache, value_cache, tail_keys, tail_values, lengths, split_slot, tail_len, parents, accepted):
    normed = layer_norm(hidden, ln_gain, ln_shift).astype(jnp.bfloat16)
    projected = jnp.einsum('sd,kdh->ksh', normed.astype(jnp.float32), qkv_weight.astype(jnp.float32)) + qkv_bias[:, None, :]
    projected = projected.reshape(3, N_GROUP, REQ, DRAFT, HEADS, HD)
    ancestry = ancestors(parents.reshape(REQS, DRAFT)).reshape(N_GROUP, REQ, DRAFT, DRAFT)
    tree_depth = lax.optimization_barrier(jnp.sum(ancestry, axis=-1)) - 1.0
    tail_grid = tail_len.reshape(N_GROUP, TAILS)
    partner_grid = tail_grid.reshape(N_GROUP // 2, 2, TAILS)[:, ::-1].reshape(N_GROUP, TAILS)
    split_table = split_slot.reshape(N_GROUP, TAILS)
    split_hot = (split_table[:, :, None] == jnp.arange(REQ, dtype=jnp.int32)[None, None, :]).astype(jnp.float32)
    extra_len = jnp.einsum('gt,gtr->gr', partner_grid.astype(jnp.float32), split_hot, precision=highest)
    length_grid = lengths.reshape(N_GROUP, REQ)
    positions = (length_grid.astype(jnp.float32) + extra_len)[:, :, None] + tree_depth
    queries = rotate(projected[0], positions).astype(jnp.bfloat16)
    keys_new = rotate(projected[1], positions).astype(jnp.bfloat16)
    values_new = projected[2].astype(jnp.bfloat16)
    cache_keys = key_cache.reshape(N_GROUP, REQ, CAP, HEADS, HD)
    cache_values = value_cache.reshape(N_GROUP, REQ, CAP, HEADS, HD)
    tail_key_grid = tail_keys.reshape(N_GROUP, TAILS, TCAP, HEADS, HD)
    tail_value_grid = tail_values.reshape(N_GROUP, TAILS, TCAP, HEADS, HD)

    def at_group(stacked, which_row):
        return lax.dynamic_index_in_dim(stacked, which_row, 0, keepdims=False)

    def attend_group(group_id):
        partner = jnp.bitwise_xor(group_id, 1)
        own_queries = at_group(queries, group_id)
        own_len = at_group(length_grid, group_id)
        own_valid = jnp.arange(CAP, dtype=jnp.int32)[None, None, :] < own_len[:, None, None]
        own_block = block_terms(own_queries, at_group(cache_keys, group_id), at_group(cache_values, group_id), own_valid)
        tree_block = block_terms(own_queries, at_group(keys_new, group_id), at_group(values_new, group_id), at_group(ancestry, group_id) > 0.5)
        split_queries = jnp.take(own_queries, at_group(split_table, group_id), axis=0)
        far_len = at_group(tail_grid, partner)
        far_valid = jnp.arange(TCAP, dtype=jnp.int32)[None, None, :] < far_len[:, None, None]
        far_block = block_terms(split_queries, at_group(tail_key_grid, partner), at_group(tail_value_grid, partner), far_valid)
        spread = spread_tails(far_block, at_group(split_hot, group_id))
        merged = combine([own_block, spread, tree_block])
        return jnp.transpose(merged, (0, 2, 1, 3)).reshape(REQ * DRAFT, HEADS * HD).astype(jnp.bfloat16)
    attended = lax.map(attend_group, jnp.arange(N_GROUP, dtype=jnp.int32)).reshape(TOKENS, HEADS * HD)
    up_lin = jnp.dot(normed, up_weight, preferred_element_type=jnp.float32) + up_bias
    activated = jax.nn.gelu(up_lin, approximate=True).astype(jnp.bfloat16)
    width_dev = HEADS * HD // N_MP
    units_dev = FF // N_MP
    summed = jnp.zeros((TOKENS, D), jnp.float32)
    for shard in range(N_MP):
        head_cols = slice(shard * width_dev, (shard + 1) * width_dev)
        unit_cols = slice(shard * units_dev, (shard + 1) * units_dev)
        branch_term = jnp.dot(attended[:, head_cols], out_weight[head_cols], preferred_element_type=jnp.float32)
        branch_term = branch_term + jnp.dot(activated[:, unit_cols], down_weight[unit_cols], preferred_element_type=jnp.float32)
        summed = summed + lax.optimization_barrier(branch_term.astype(jnp.bfloat16)).astype(jnp.float32)
    new_hidden = (hidden.astype(jnp.float32) + summed + branch_bias).astype(jnp.bfloat16)
    next_normed = layer_norm(new_hidden, next_gain, next_shift).astype(jnp.bfloat16)
    next_qkv = jnp.einsum('sd,kdh->ksh', next_normed.astype(jnp.float32), next_weight.astype(jnp.float32)) + next_bias[:, None, :]
    next_qkv = next_qkv.astype(jnp.bfloat16)
    keys_flat = keys_new.reshape(REQS, DRAFT, HEADS * HD)
    values_flat = values_new.reshape(REQS, DRAFT, HEADS * HD)
    picked_keys = jnp.take_along_axis(keys_flat, accepted[:, :, None], axis=1).reshape(REQS * ACC, HEADS * HD)
    picked_values = jnp.take_along_axis(values_flat, accepted[:, :, None], axis=1).reshape(REQS * ACC, HEADS * HD)
    return (new_hidden, next_qkv, jnp.stack([picked_keys, picked_values]))
```

```python
import functools
from types import SimpleNamespace

import jax
import jax.numpy as jnp
import numpy as np
from jax import lax
from jax.experimental import pallas as pl
from jax.experimental.pallas import tpu as pltpu
from jax.sharding import PartitionSpec as P

HD = 64
ROT = 32
DRAFT = 64
PAIR = 128
BLOCK = 512
STEP = 16

KEPT = tuple(dict(w_qkv=0, w_up=0, w_down=0, w_out=0))
FREE = tuple(dict(far_keys=0, far_values=0)) + tuple(range(20))

epsilon = 1e-05
very_low = -1e30

HBM = pltpu.HBM
VMEM = pltpu.VMEM
SMEM = pltpu.SMEM
I32 = jnp.int32
F32 = jnp.float32
BF16 = jnp.bfloat16

CHUNKS = (((0, 1),), ((2, 3),), ((4, 5),), ((6,), (7,)))
FINISHES = ((0, 3), (3, 4), (4, 5))


def dot(a, b):
    return jnp.dot(a, b, preferred_element_type=F32)


def dot_nt(a, b):
    return lax.dot_general(a, b, (((1,), (1,)), ((), ())), preferred_element_type=F32)


def request_at(place, slots, requests):
    tails = slots.shape[0]
    whole = requests - tails
    if place >= whole:
        return slots[place - whole]
    ordered = [slots[t] for t in range(tails)]
    for end in range(tails - 1, 0, -1):
        for t in range(end):
            low = jnp.minimum(ordered[t], ordered[t + 1])
            high = jnp.maximum(ordered[t], ordered[t + 1])
            ordered[t], ordered[t + 1] = low, high
    request = jnp.int32(place)
    for slot in ordered:
        request = request + (request >= slot).astype(I32)
    return request


class Copies:
    def __init__(self, sems):
        self.sems = sems
        self.used = 0

    def make(self, source, target):
        copy = pltpu.make_async_copy(source, target, self.sems.at[self.used])
        self.used += 1
        return copy

    def start(self, source, target):
        copy = self.make(source, target)
        copy.start()
        return copy


def wait(*copies):
    for copy in copies:
        copy.wait()


def layer_norm(values, gain, shift):
    centred = values - jnp.mean(values, axis=-1, keepdims=True)
    variance = jnp.mean(centred * centred, axis=-1, keepdims=True)
    return centred * lax.rsqrt(variance + epsilon) * gain + shift


def ancestor_pair(parents, first, second):
    lane = lax.broadcasted_iota(I32, (1, PAIR), 1)

    def row_of(request, half):
        row = parents[pl.ds(request // 2, 1), :]
        return jnp.where(request % 2 == half, row, pltpu.roll(row, DRAFT, 1))

    ids = jnp.where(lane < DRAFT, row_of(first, 0), row_of(second, 1) + DRAFT)
    row_id = lax.broadcasted_iota(I32, (PAIR, PAIR), 0)
    col_id = lax.broadcasted_iota(I32, (PAIR, PAIR), 1)
    below = jnp.where(row_id == ids, 1.0, 0.0).astype(BF16)
    same = jnp.where(row_id == col_id, 1.0, 0.0).astype(BF16)
    reach = jnp.minimum(dot_nt(same, below) + same.astype(F32), 1.0)
    for _ in range((DRAFT - 1).bit_length()):
        half = reach.astype(BF16)
        reach = jnp.minimum(dot(half, half), 1.0)
    return reach


def rotary_tables(positions):
    feature = lax.broadcasted_iota(I32, (1, PAIR), 1) % HD
    inverse = jnp.zeros((1, PAIR), F32)
    for k in range(ROT // 2):
        rate = float(np.float32(10000.0 ** (-k * 2.0 / ROT)))
        inverse = jnp.where(feature % (ROT // 2) == k, rate, inverse)
    angles = positions * inverse
    sine = jnp.sin(angles)
    same = jnp.where(feature < ROT, jnp.cos(angles), 1.0)
    ahead = jnp.where(feature < ROT // 2, -sine, 0.0)
    behind = jnp.where((feature >= ROT // 2) & (feature < ROT), sine, 0.0)
    return same, ahead, behind


def rotate(values, tables):
    same, ahead, behind = tables
    half_rot = ROT // 2
    parts = []
    for start in range(0, values.shape[1], PAIR):
        part = values[:, start : start + PAIR]
        parts.append(
            part * same
            + pltpu.roll(part, PAIR - half_rot, 1) * ahead
            + pltpu.roll(part, half_rot, 1) * behind
        )
    return jnp.concatenate(parts, axis=1) if len(parts) > 1 else parts[0]


def gelu(v):
    inner = np.float32(np.sqrt(2.0 / np.pi)) * (v + 0.044715 * (v * v * v))
    return 0.5 * v * (1.0 + jnp.tanh(inner))


def picks(accepted, request, tokens):
    count = accepted.shape[1]
    row = accepted[pl.ds(request, 1), :]
    row_id = lax.broadcasted_iota(I32, (count, count), 0)
    col_id = lax.broadcasted_iota(I32, (count, count), 1)
    ids = jnp.sum(jnp.where(row_id == col_id, row, 0).astype(F32), axis=1, keepdims=True)
    token_id = lax.broadcasted_iota(I32, (count, tokens), 1).astype(F32)
    return jnp.where(token_id == ids, 1.0, 0.0).astype(BF16)


def branch_kernel(pieces, first, names, *refs):
    r = SimpleNamespace(**dict(zip(names, refs)))
    places = [place for piece in pieces for place in piece]
    count = len(places)
    rows = count * DRAFT
    requests, _, width = r.hidden.shape
    heads_width = r.w_qkv.shape[2]
    units = r.w_up.shape[1]
    cap_len = r.key_cache.shape[1]
    tails = r.split_slot.shape[0]
    whole = requests - tails
    group = min(heads_width, 4 * HD)
    per = group // HD
    copies = Copies(r.sems)

    got_scalars = [
        copies.start(r.split_slot, r.slots),
        copies.start(r.lengths, r.own_len),
        copies.start(r.tail_len, r.all_len),
    ]
    got_small = [
        copies.start(r.parents, r.tree),
        copies.start(r.accepted, r.taken),
        copies.start(r.ln_gain, r.gain),
        copies.start(r.ln_shift, r.shift),
        copies.start(r.qkv_bias, r.b_qkv),
        copies.start(r.up_bias, r.b_up),
    ]
    early = places[-1] < whole
    if early:
        span = pl.ds(places[0], places[-1] - places[0] + 1 + tails)
        got_hidden = [copies.start(r.hidden.at[span], r.h)]
    got_qkv = [copies.start(r.qkv_weight.at[c], r.w_qkv.at[c]) for c in range(3)] if first else []
    wait(*got_scalars)
    order = [request_at(place, r.slots, requests) for place in places]
    far_base = jnp.bitwise_xor(lax.axis_index("group"), 1) * tails
    if not early:
        got_hidden = [copies.start(r.hidden.at[order[i]], r.h.at[i]) for i in range(count)]
        rows_of = range(count)
    else:
        rows_of = [request - places[0] for request in order]
    got_own = [
        (
            copies.start(r.key_cache.at[order[i]], r.k_own.at[i]),
            copies.start(r.value_cache.at[order[i]], r.v_own.at[i]),
        )
        for i in range(count)
    ]
    up_blocks = range(0, units, BLOCK)
    down_blocks = range(0, width, BLOCK)
    if first:
        got_up = [
            copies.start(r.up_weight.at[:, pl.ds(b, BLOCK)], r.w_up.at[:, pl.ds(b, BLOCK)])
            for b in up_blocks
        ]
        got_out = copies.start(r.out_weight, r.w_out)
        got_down = [
            copies.start(r.down_weight.at[:, pl.ds(b, BLOCK)], r.w_down.at[:, pl.ds(b, BLOCK)])
            for b in down_blocks
        ]
    if places[-1] >= whole:
        got_far = [
            (copies.start(r.far_keys.at[t], r.k_far.at[t]), copies.start(r.far_values.at[t], r.v_far.at[t]))
            for t in range(tails)
        ]

    wait(*got_small)
    reach = []
    tables = []
    for i in range(0, count, 2):
        both = ancestor_pair(r.tree, order[i], order[i + 1])
        depth = jnp.sum(both, axis=1, keepdims=True) - 1.0
        for k in (0, 1):
            span = slice(k * DRAFT, (k + 1) * DRAFT)
            reach.append(both[span, span])
            base = r.own_len[order[i + k]].astype(F32)
            if places[i + k] >= whole:
                base = base + r.all_len[far_base + places[i + k] - whole].astype(F32)
            tables.append(rotary_tables(base + depth[span]))

    wait(*got_hidden)
    gain = r.gain[...]
    shift = r.shift[...]

    for i in range(count):
        for k in range(0, DRAFT, STEP):
            values = r.h[rows_of[i], pl.ds(k, STEP), :].astype(F32)
            r.normed[pl.ds(i * DRAFT + k, STEP), :] = layer_norm(values, gain, shift).astype(BF16)

    for c, target in enumerate((r.q, r.k, r.v)):
        wait(*got_qkv[c : c + 1])
        linear = dot(r.normed[...], r.w_qkv[c]) + r.b_qkv[pl.ds(c, 1), :]
        for i in range(count):
            part = linear[i * DRAFT : (i + 1) * DRAFT]
            if c < 2:
                part = rotate(part, tables[i])
            part = part.astype(BF16)
            if c == 0:
                part = part * np.float32(HD**-0.5).astype(BF16)
            target[pl.ds(i * DRAFT, DRAFT), :] = part

    writes = []
    for i in range(count):
        hot = picks(r.taken, order[i], DRAFT)
        for c, source in enumerate((r.k, r.v)):
            r.picked[c, i] = dot(hot, source[pl.ds(i * DRAFT, DRAFT), :]).astype(BF16)
            writes.append(copies.start(r.picked.at[c, i], r.rows_out.at[c, order[i]]))

    lane_head = lax.broadcasted_iota(I32, (DRAFT, group), 1) // HD
    for i in range(count):
        wait(*got_own[i])
        t = places[i] - whole
        if t >= 0:
            wait(*got_far[t])
        span = pl.ds(i * DRAFT, DRAFT)
        key_id = lax.broadcasted_iota(I32, (1, cap_len), 1)
        own_bias = jnp.where(key_id < r.own_len[order[i]], 0.0, very_low)
        tree_bias = jnp.where(reach[i] > 0.5, 0.0, very_low)
        tree_bias = jnp.concatenate([tree_bias] * per, axis=0)
        for low in range(0, heads_width, group):
            cols = slice(low, low + group)
            query = r.q[span, cols]
            query = jnp.concatenate(
                [jnp.where(lane_head == h, query, jnp.zeros_like(query)) for h in range(per)], axis=0
            )
            own = dot_nt(query, r.k_own[i, :, cols]) + own_bias
            tree = dot_nt(query, r.k[span, cols]) + tree_bias
            top = jnp.maximum(
                jnp.max(own, axis=1, keepdims=True), jnp.max(tree, axis=1, keepdims=True)
            )
            own = jnp.exp(own - top)
            tree = jnp.exp(tree - top)
            total = jnp.sum(own, axis=1, keepdims=True) + jnp.sum(tree, axis=1, keepdims=True)
            mixed = dot(own.astype(BF16), r.v_own[i, :, cols])
            mixed = mixed + dot(tree.astype(BF16), r.v[span, cols])
            if t >= 0:
                far_cap = r.k_far.shape[1]
                far_len = r.all_len[far_base + t]
                for start in range(0, far_cap, BLOCK):
                    part = slice(start, start + BLOCK)
                    far_id = lax.broadcasted_iota(I32, (1, BLOCK), 1) + start
                    far_bias = jnp.where(far_id < far_len, 0.0, very_low)
                    far = dot_nt(query, r.k_far[t, part, cols]) + far_bias
                    peak = jnp.maximum(top, jnp.max(far, axis=1, keepdims=True))
                    keep = jnp.exp(top - peak)
                    far = jnp.exp(far - peak)
                    total = total * keep + jnp.sum(far, axis=1, keepdims=True)
                    mixed = mixed * keep + dot(far.astype(BF16), r.v_far[t, part, cols])
                    top = peak
            mixed = mixed * (1.0 / total)
            joined = jnp.zeros((DRAFT, group), F32)
            for h in range(per):
                joined = jnp.where(lane_head == h, mixed[h * DRAFT : (h + 1) * DRAFT], joined)
            r.att[span, cols] = joined.astype(BF16)

    for n, b in enumerate(up_blocks):
        if first:
            wait(got_up[n])
        cols = pl.ds(b, BLOCK)
        r.act[:, cols] = gelu(dot(r.normed[...], r.w_up[:, cols]) + r.b_up[:, cols]).astype(BF16)
    if first:
        wait(got_out)
    for n, b in enumerate(down_blocks):
        cols = pl.ds(b, BLOCK)
        summed = dot(r.att[...], r.w_out[:, cols])
        if first:
            wait(got_down[n])
        r.sums[:, cols] = (summed + dot(r.act[...], r.w_down[:, cols])).astype(BF16)
        start = 0
        for piece, target in zip(pieces, (getattr(r, n) for n in names if n.startswith("piece"))):
            size = len(piece) * DRAFT
            writes.append(copies.start(r.sums.at[pl.ds(start, size), cols], target.at[:, cols]))
            start += size
    wait(*writes)


def call(kernel, ins, outs, scratch, aliases, vmem, name):
    names = (*ins, *outs, *scratch)
    results = pl.pallas_call(
        functools.partial(kernel, names),
        out_shape=[(VMEM if key in KEPT else HBM)(shape, BF16) for key, shape in outs.items()],
        in_specs=[
            pl.BlockSpec(memory_space=VMEM if key in KEPT else pl.ANY if key in FREE else HBM) for key in ins
        ],
        out_specs=[pl.BlockSpec(memory_space=VMEM if key in KEPT else HBM) for key in outs],
        scratch_shapes=list(scratch.values()),
        input_output_aliases={list(ins).index(a): list(outs).index(b) for a, b in aliases.items()},
        compiler_params=pltpu.CompilerParams(vmem_limit_bytes=vmem * 2**20),
        name=name,
    )(*(x if key in FREE else pltpu.with_memory_space_constraint(x, VMEM if key in KEPT else HBM) for key, x in ins.items()))
    return SimpleNamespace(**dict(zip(outs, results)))


def branch(pieces, tail, a, before):
    requests, _, width = a.hidden.shape
    heads_width = a.qkv_weight.shape[2]
    units = a.up_weight.shape[1]
    cap_len = a.key_cache.shape[1]
    acc_count = a.accepted.shape[1]
    tails = a.split_slot.shape[0]
    count = sum(len(piece) for piece in pieces)
    rows = count * DRAFT
    ins = dict(
        lengths=a.lengths,
        split_slot=a.split_slot,
        tail_len=a.tail_len,
        accepted=a.accepted,
        parents=a.parents,
        ln_gain=a.ln_gain,
        ln_shift=a.ln_shift,
        qkv_bias=a.qkv_bias,
        up_bias=a.up_bias,
        hidden=a.hidden,
        key_cache=a.key_cache,
        value_cache=a.value_cache,
    )
    scratch = dict(
        slots=SMEM(a.split_slot.shape, I32),
        own_len=SMEM(a.lengths.shape, I32),
        all_len=SMEM(a.tail_len.shape, I32),
        tree=VMEM(a.parents.shape, I32),
        taken=VMEM(a.accepted.shape, I32),
        gain=VMEM((1, width), F32),
        shift=VMEM((1, width), F32),
        b_qkv=VMEM((3, heads_width), F32),
        b_up=VMEM((1, units), F32),
        h=VMEM((count + (0 if tail else tails), DRAFT, width), BF16),
        normed=VMEM((rows, width), BF16),
        k_own=VMEM((count, cap_len, heads_width), BF16),
        v_own=VMEM((count, cap_len, heads_width), BF16),
        q=VMEM((rows, heads_width), BF16),
        k=VMEM((rows, heads_width), BF16),
        v=VMEM((rows, heads_width), BF16),
        att=VMEM((rows, heads_width), BF16),
        act=VMEM((rows, units), BF16),
        sums=VMEM((rows, width), BF16),
        picked=VMEM((2, count, acc_count, heads_width), BF16),
        sems=pltpu.SemaphoreType.DMA((100,)),
    )
    if tail:
        ins.update(far_keys=a.far_keys, far_values=a.far_values)
        scratch.update(k_far=VMEM(a.far_keys.shape, BF16), v_far=VMEM(a.far_values.shape, BF16))
    outs = dict(rows_out=(2, requests, acc_count, heads_width))
    aliases = {}
    if before is None:
        ins.update(
            qkv_weight=a.qkv_weight, up_weight=a.up_weight, down_weight=a.down_weight, out_weight=a.out_weight
        )
        outs.update(
            w_qkv=a.qkv_weight.shape, w_up=a.up_weight.shape, w_down=a.down_weight.shape, w_out=a.out_weight.shape
        )
    else:
        ins.update(
            rows_in=before.rows_out, w_qkv=a.w_qkv, w_up=a.w_up, w_down=a.w_down, w_out=a.w_out
        )
        aliases = dict(rows_in="rows_out")
    sizes = [len(piece) * DRAFT for piece in pieces]
    if len(sizes) == 1:
        outs.update(piece_a=(sizes[0], width))
    else:
        outs.update(piece_a=(sizes[0], width), piece_b=(sizes[1], width))

    def kernel(names, *refs):
        branch_kernel(pieces, before is None, names, *refs)

    out = call(kernel, ins, outs, scratch, aliases, 36, "branch")
    parts = [out.piece_a] if len(sizes) == 1 else [out.piece_a, out.piece_b]
    if before is None:
        a.w_qkv, a.w_up, a.w_down, a.w_out = out.w_qkv, out.w_up, out.w_down, out.w_out
    return parts, out


def finish_kernel(pieces, terms, names, *refs):
    r = SimpleNamespace(**{str(name): ref for name, ref in zip(names, refs)})
    requests, _, width = r.hidden.shape
    share = r.new_hidden.shape[0]
    places = [place for piece in pieces for place in piece]
    count = len(places)
    copies = Copies(r.sems)
    wait_slots = copies.start(r.split_slot, r.slots)
    got_terms = []
    given = iter(refs)
    for n in range(terms):
        start = 0
        for piece in pieces:
            size = len(piece) * DRAFT
            got_terms.append(copies.start(next(given), r.t.at[n, pl.ds(start, size)]))
            start += size
    got_small = [
        copies.start(r.branch_bias, r.bias),
        copies.start(r.next_gain, r.gain),
        copies.start(r.next_shift, r.shift),
        copies.start(r.next_bias, r.b),
    ]
    wait(wait_slots)
    order = [request_at(place, r.slots, requests) for place in places]
    got_hidden = [
        copies.start(r.hidden.at[order[i]], r.h.at[pl.ds(i * DRAFT, DRAFT)]) for i in range(count)
    ]
    got_w = [copies.start(r.next_weight.at[c], r.w.at[c]) for c in range(3)]
    wait(*got_terms, *got_small, *got_hidden)
    bias = r.bias[...]
    gain = r.gain[...]
    shift = r.shift[...]

    def body(k, carry):
        at = pl.ds(pl.multiple_of(k * STEP, STEP), STEP)
        summed = r.t[0, at, :].astype(F32)
        for n in range(1, terms):
            summed = summed + r.t[n, at, :].astype(F32)
        new = (r.h[at, :].astype(F32) + summed + bias).astype(BF16)
        r.h[at, :] = new
        r.normed[at, :] = layer_norm(new.astype(F32), gain, shift).astype(BF16)
        return carry

    lax.fori_loop(0, count * DRAFT // STEP, body, 0, unroll=4)

    rank = lax.axis_index("mp")
    new_writes = []
    for i in range(count):
        copy = copies.make(r.h.at[pl.ds(i * DRAFT, DRAFT)], r.new_hidden.at[order[i] % share])
        owned = order[i] // share == rank
        new_writes.append((owned, copy))
        pl.when(owned)(copy.start)
    writes = []
    for c in range(3):
        wait(got_w[c])
        linear = (dot(r.normed[...], r.w[c]) + r.b[pl.ds(c, 1), :]).astype(BF16)
        for i in range(count):
            r.o[c, i] = linear[i * DRAFT : (i + 1) * DRAFT]
            writes.append(copies.start(r.o.at[c, i], r.next_qkv.at[c, order[i]]))
    wait(*writes)
    for owned, copy in new_writes:
        pl.when(owned)(copy.wait)


def finish(sent, a, last):
    requests, _, width = a.hidden.shape
    heads_width = a.next_weight.shape[2]
    share = requests // a.n_mp
    pieces = [piece for piece, _ in sent]
    count = sum(len(piece) for piece in pieces)
    rows = count * DRAFT
    terms = len(sent[0][1])
    ins = {}
    for n in range(terms):
        for _, parts in sent:
            ins[len(ins)] = parts[n]
    ins.update(
        split_slot=a.split_slot,
        branch_bias=a.branch_bias,
        next_gain=a.next_gain,
        next_shift=a.next_shift,
        next_bias=a.next_bias,
        hidden=a.hidden,
        next_weight=a.next_weight,
    )
    aliases = {}
    if last is not None:
        ins.update(new_in=last.new_hidden, qkv_in=last.next_qkv)
        aliases = dict(new_in="new_hidden", qkv_in="next_qkv")
    outs = dict(new_hidden=(share, DRAFT, width), next_qkv=(3, requests, DRAFT, heads_width))
    scratch = dict(
        slots=SMEM(a.split_slot.shape, I32),
        bias=VMEM((1, width), F32),
        gain=VMEM((1, width), F32),
        shift=VMEM((1, width), F32),
        b=VMEM((3, heads_width), F32),
        h=VMEM((rows, width), BF16),
        t=VMEM((terms, rows, width), BF16),
        normed=VMEM((rows, width), BF16),
        w=VMEM((3, width, heads_width), BF16),
        o=VMEM((3, count, DRAFT, heads_width), BF16),
        sems=pltpu.SemaphoreType.DMA((60,)),
    )

    def kernel(names, *refs):
        finish_kernel(pieces, terms, names, *refs)

    return call(kernel, ins, outs, scratch, aliases, 60, "finish")


def local(
    hidden,
    ln_gain,
    ln_shift,
    qkv_weight,
    qkv_bias,
    out_weight,
    up_weight,
    up_bias,
    down_weight,
    branch_bias,
    next_gain,
    next_shift,
    next_weight,
    next_bias,
    key_cache,
    value_cache,
    tail_keys,
    tail_values,
    lengths,
    split_slot,
    tail_len,
    parents,
    accepted,
):
    requests = lengths.shape[0]
    width = hidden.shape[1]
    n_mp = lax.axis_size("mp")
    groups = lax.axis_size("group")
    a = SimpleNamespace(
        hidden=hidden.reshape(requests, DRAFT, width),
        ln_gain=ln_gain.reshape(1, width),
        ln_shift=ln_shift.reshape(1, width),
        qkv_weight=qkv_weight,
        qkv_bias=qkv_bias,
        out_weight=out_weight,
        up_weight=up_weight,
        up_bias=up_bias.reshape(1, -1),
        down_weight=down_weight,
        branch_bias=branch_bias.reshape(1, width),
        next_gain=next_gain.reshape(1, width),
        next_shift=next_shift.reshape(1, width),
        next_weight=next_weight,
        next_bias=next_bias,
        key_cache=key_cache,
        value_cache=value_cache,
        lengths=lengths,
        split_slot=split_slot,
        tail_len=tail_len,
        parents=parents.reshape(requests * DRAFT // PAIR, PAIR),
        accepted=accepted,
        n_mp=n_mp,
    )
    out = None
    sent = []
    for k, pieces in enumerate(CHUNKS):
        if k == 1:
            tail_keys, tail_values, _ = lax.optimization_barrier((tail_keys, tail_values, sent[0][1][0]))
            swap = [(i, i ^ 1) for i in range(groups)]
            a.far_keys, a.far_values = lax.ppermute((tail_keys, tail_values), "group", swap)
        if k >= 2:
            a.lengths, _ = lax.optimization_barrier((a.lengths, sent[k - 2][1][-1]))
        sums, out = branch(pieces, k == len(CHUNKS) - 1, a, out)
        for piece, part in zip(pieces, sums):
            if n_mp == 2:
                sent.append((piece, (part, lax.ppermute(part, "mp", [(0, 1), (1, 0)]))))
            else:
                sent.append((piece, (lax.psum(part, "mp"),)))
    a.branch_bias, _ = lax.optimization_barrier((a.branch_bias, sums))
    last = None
    for first, end in FINISHES:
        last = finish(sent[first:end], a, last)
    heads_width = qkv_weight.shape[2]
    return (
        last.new_hidden.reshape(-1, width),
        last.next_qkv.reshape(3, requests * DRAFT, heads_width),
        out.rows_out.reshape(2, -1, heads_width),
    )


def solution(mesh):
    in_specs = (
        P("group", None),
        P(),
        P(),
        P(None, None, "mp"),
        P(None, "mp"),
        P("mp", None),
        P(None, "mp"),
        P("mp"),
        P("mp", None),
        P(),
        P(),
        P(),
        P(None, None, "mp"),
        P(None, "mp"),
        P("group", None, "mp"),
        P("group", None, "mp"),
        P("group", None, "mp"),
        P("group", None, "mp"),
        P("group"),
        P("group"),
        P(),
        P("group"),
        P("group", None),
    )
    out_specs = (P(("group", "mp"), None), P(None, "group", "mp"), P(None, "group", "mp"))
    return jax.shard_map(local, mesh=mesh, in_specs=in_specs, out_specs=out_specs, check_vma=False)
```

```python
import functools
from types import SimpleNamespace

import jax
import jax.numpy as jnp
import numpy as np
from jax import lax
from jax.experimental import pallas as pl
from jax.experimental.pallas import tpu as pltpu
from jax.sharding import PartitionSpec as P

HD = 64
ROT = 32
DRAFT = 64
PAIR = 128
BLOCK = 512
STEP = 16
VMEM_MIB = 35

epsilon = 1e-05
very_low = -1e30

HBM = pltpu.HBM
VMEM = pltpu.VMEM
SMEM = pltpu.SMEM
I32 = jnp.int32
F32 = jnp.float32
BF16 = jnp.bfloat16

CHUNKS = (((0, 1),), ((2, 3),), ((4, 5),), ((6,), (7,)))
FINISHES = ((0, 3), (3, 4), (4, 5))


def dot(a, b):
    return jnp.dot(a, b, preferred_element_type=F32)


def dot_nt(a, b):
    return lax.dot_general(a, b, (((1,), (1,)), ((), ())), preferred_element_type=F32)


def request_at(place, slots, requests):
    tails = slots.shape[0]
    whole = requests - tails
    if place >= whole:
        return slots[place - whole]
    ordered = [slots[t] for t in range(tails)]
    for end in range(tails - 1, 0, -1):
        for t in range(end):
            low = jnp.minimum(ordered[t], ordered[t + 1])
            high = jnp.maximum(ordered[t], ordered[t + 1])
            ordered[t], ordered[t + 1] = low, high
    request = jnp.int32(place)
    for slot in ordered:
        request = request + (request >= slot).astype(I32)
    return request


class Copies:
    def __init__(self, sems):
        self.sems = sems
        self.used = 0

    def make(self, source, target):
        copy = pltpu.make_async_copy(source, target, self.sems.at[self.used])
        self.used += 1
        return copy

    def start(self, source, target):
        copy = self.make(source, target)
        copy.start()
        return copy


def wait(*copies):
    for copy in copies:
        copy.wait()


def layer_norm(values, gain, shift):
    centred = values - jnp.mean(values, axis=-1, keepdims=True)
    variance = jnp.mean(centred * centred, axis=-1, keepdims=True)
    return centred * lax.rsqrt(variance + epsilon) * gain + shift


def ancestor_pair(parents, first, second):
    lane = lax.broadcasted_iota(I32, (1, PAIR), 1)

    def row_of(request, half):
        row = parents[pl.ds(request // 2, 1), :]
        return jnp.where(request % 2 == half, row, pltpu.roll(row, DRAFT, 1))

    ids = jnp.where(lane < DRAFT, row_of(first, 0), row_of(second, 1) + DRAFT)
    row_id = lax.broadcasted_iota(I32, (PAIR, PAIR), 0)
    col_id = lax.broadcasted_iota(I32, (PAIR, PAIR), 1)
    below = jnp.where(row_id == ids, 1.0, 0.0).astype(BF16)
    same = jnp.where(row_id == col_id, 1.0, 0.0).astype(BF16)
    reach = jnp.minimum(dot_nt(same, below) + same.astype(F32), 1.0)
    for _ in range((DRAFT - 1).bit_length()):
        half = reach.astype(BF16)
        reach = jnp.minimum(dot(half, half), 1.0)
    return reach


def rotary_tables(positions):
    feature = lax.broadcasted_iota(I32, (1, PAIR), 1) % HD
    inverse = jnp.zeros((1, PAIR), F32)
    for k in range(ROT // 2):
        rate = float(np.float32(10000.0 ** (-k * 2.0 / ROT)))
        inverse = jnp.where(feature % (ROT // 2) == k, rate, inverse)
    angles = positions * inverse
    sine = jnp.sin(angles)
    same = jnp.where(feature < ROT, jnp.cos(angles), 1.0)
    ahead = jnp.where(feature < ROT // 2, -sine, 0.0)
    behind = jnp.where((feature >= ROT // 2) & (feature < ROT), sine, 0.0)
    return same, ahead, behind


def rotate(values, tables):
    same, ahead, behind = tables
    half_rot = ROT // 2
    parts = []
    for start in range(0, values.shape[1], PAIR):
        part = values[:, start : start + PAIR]
        parts.append(
            part * same
            + pltpu.roll(part, PAIR - half_rot, 1) * ahead
            + pltpu.roll(part, half_rot, 1) * behind
        )
    return jnp.concatenate(parts, axis=1) if len(parts) > 1 else parts[0]


def gelu(v):
    inner = np.float32(np.sqrt(2.0 / np.pi)) * (v + 0.044715 * (v * v * v))
    return 0.5 * v * (1.0 + jnp.tanh(inner))


def picks(accepted, request, tokens):
    count = accepted.shape[1]
    row = accepted[pl.ds(request, 1), :]
    row_id = lax.broadcasted_iota(I32, (count, count), 0)
    col_id = lax.broadcasted_iota(I32, (count, count), 1)
    ids = jnp.sum(jnp.where(row_id == col_id, row, 0).astype(F32), axis=1, keepdims=True)
    token_id = lax.broadcasted_iota(I32, (count, tokens), 1).astype(F32)
    return jnp.where(token_id == ids, 1.0, 0.0).astype(BF16)


def branch_kernel(pieces, first, add_own, names, *refs):
    r = SimpleNamespace(**dict(zip(names, refs)))
    places = [place for piece in pieces for place in piece]
    count = len(places)
    rows = count * DRAFT
    requests, _, width = r.hidden.shape
    heads_width = r.w_qkv.shape[2]
    units = r.w_up.shape[1]
    cap_len = r.key_cache.shape[1]
    tails = r.split_slot.shape[0]
    whole = requests - tails
    group = min(heads_width, 4 * HD)
    per = group // HD
    copies = Copies(r.sems)

    got_scalars = [
        copies.start(r.split_slot, r.slots),
        copies.start(r.lengths, r.own_len),
        copies.start(r.tail_len, r.all_len),
    ]
    got_small = [
        copies.start(r.parents, r.tree),
        copies.start(r.accepted, r.taken),
        copies.start(r.ln_gain, r.gain),
        copies.start(r.ln_shift, r.shift),
        copies.start(r.qkv_bias, r.b_qkv),
        copies.start(r.up_bias, r.b_up),
        copies.start(r.branch_bias, r.bias),
    ]
    early = places[-1] < whole
    if early:
        span = pl.ds(places[0], places[-1] - places[0] + 1 + tails)
        got_hidden = [copies.start(r.hidden.at[span], r.h)]
    got_qkv = [copies.start(r.qkv_weight.at[c], r.w_qkv.at[c]) for c in range(3)] if first else []
    wait(*got_scalars)
    order = [request_at(place, r.slots, requests) for place in places]
    far_base = jnp.bitwise_xor(lax.axis_index("group"), 1) * tails
    if not early:
        got_hidden = [copies.start(r.hidden.at[order[i]], r.h.at[i]) for i in range(count)]
        rows_of = range(count)
    else:
        rows_of = [request - places[0] for request in order]
    got_own = [
        (
            copies.start(r.key_cache.at[order[i]], r.k_own.at[i]),
            copies.start(r.value_cache.at[order[i]], r.v_own.at[i]),
        )
        for i in range(count)
    ]
    up_blocks = range(0, units, BLOCK)
    down_blocks = range(0, width, BLOCK)
    if first:
        got_up = [
            copies.start(r.up_weight.at[:, pl.ds(b, BLOCK)], r.w_up.at[:, pl.ds(b, BLOCK)])
            for b in up_blocks
        ]
        got_out = copies.start(r.out_weight, r.w_out)
        got_down = [
            copies.start(r.down_weight.at[:, pl.ds(b, BLOCK)], r.w_down.at[:, pl.ds(b, BLOCK)])
            for b in down_blocks
        ]
    if places[-1] >= whole:
        got_far = [
            (copies.start(r.far_keys.at[t], r.k_far.at[t]), copies.start(r.far_values.at[t], r.v_far.at[t]))
            for t in range(tails)
        ]

    wait(*got_small)
    reach = []
    tables = []
    for i in range(0, count, 2):
        both = ancestor_pair(r.tree, order[i], order[i + 1])
        depth = jnp.sum(both, axis=1, keepdims=True) - 1.0
        for k in (0, 1):
            span = slice(k * DRAFT, (k + 1) * DRAFT)
            reach.append(both[span, span])
            base = r.own_len[order[i + k]].astype(F32)
            if places[i + k] >= whole:
                base = base + r.all_len[far_base + places[i + k] - whole].astype(F32)
            tables.append(rotary_tables(base + depth[span]))

    wait(*got_hidden)
    gain = r.gain[...]
    shift = r.shift[...]

    for i in range(count):
        for k in range(0, DRAFT, STEP):
            values = r.h[rows_of[i], pl.ds(k, STEP), :].astype(F32)
            r.normed[pl.ds(i * DRAFT + k, STEP), :] = layer_norm(values, gain, shift).astype(BF16)

    for c, target in enumerate((r.q, r.k, r.v)):
        wait(*got_qkv[c : c + 1])
        linear = dot(r.normed[...], r.w_qkv[c]) + r.b_qkv[pl.ds(c, 1), :]
        for i in range(count):
            part = linear[i * DRAFT : (i + 1) * DRAFT]
            if c < 2:
                part = rotate(part, tables[i])
            part = part.astype(BF16)
            if c == 0:
                part = part * np.float32(HD**-0.5).astype(BF16)
            target[pl.ds(i * DRAFT, DRAFT), :] = part

    writes = []
    for i in range(count):
        hot = picks(r.taken, order[i], DRAFT)
        for c, source in enumerate((r.k, r.v)):
            r.picked[c, i] = dot(hot, source[pl.ds(i * DRAFT, DRAFT), :]).astype(BF16)
            writes.append(copies.start(r.picked.at[c, i], r.rows_out.at[c, order[i]]))

    lane_head = lax.broadcasted_iota(I32, (DRAFT, group), 1) // HD
    for i in range(count):
        wait(*got_own[i])
        t = places[i] - whole
        if t >= 0:
            wait(*got_far[t])
        span = pl.ds(i * DRAFT, DRAFT)
        key_id = lax.broadcasted_iota(I32, (1, cap_len), 1)
        own_bias = jnp.where(key_id < r.own_len[order[i]], 0.0, very_low)
        tree_bias = jnp.where(reach[i] > 0.5, 0.0, very_low)
        tree_bias = jnp.concatenate([tree_bias] * per, axis=0)
        for low in range(0, heads_width, group):
            cols = slice(low, low + group)
            query = r.q[span, cols]
            query = jnp.concatenate(
                [jnp.where(lane_head == h, query, jnp.zeros_like(query)) for h in range(per)], axis=0
            )
            own = dot_nt(query, r.k_own[i, :, cols]) + own_bias
            tree = dot_nt(query, r.k[span, cols]) + tree_bias
            top = jnp.maximum(
                jnp.max(own, axis=1, keepdims=True), jnp.max(tree, axis=1, keepdims=True)
            )
            own = jnp.exp(own - top)
            tree = jnp.exp(tree - top)
            total = jnp.sum(own, axis=1, keepdims=True) + jnp.sum(tree, axis=1, keepdims=True)
            mixed = dot(own.astype(BF16), r.v_own[i, :, cols])
            mixed = mixed + dot(tree.astype(BF16), r.v[span, cols])
            if t >= 0:
                far_cap = r.k_far.shape[1]
                far_len = r.all_len[far_base + t]
                for start in range(0, far_cap, BLOCK):
                    part = slice(start, start + BLOCK)
                    far_id = lax.broadcasted_iota(I32, (1, BLOCK), 1) + start
                    far_bias = jnp.where(far_id < far_len, 0.0, very_low)
                    far = dot_nt(query, r.k_far[t, part, cols]) + far_bias
                    peak = jnp.maximum(top, jnp.max(far, axis=1, keepdims=True))
                    keep = jnp.exp(top - peak)
                    far = jnp.exp(far - peak)
                    total = total * keep + jnp.sum(far, axis=1, keepdims=True)
                    mixed = mixed * keep + dot(far.astype(BF16), r.v_far[t, part, cols])
                    top = peak
            mixed = mixed * (1.0 / total)
            joined = jnp.zeros((DRAFT, group), F32)
            for h in range(per):
                joined = jnp.where(lane_head == h, mixed[h * DRAFT : (h + 1) * DRAFT], joined)
            r.att[span, cols] = joined.astype(BF16)

    for n, b in enumerate(up_blocks):
        if first:
            wait(got_up[n])
        cols = pl.ds(b, BLOCK)
        r.act[:, cols] = gelu(dot(r.normed[...], r.w_up[:, cols]) + r.b_up[:, cols]).astype(BF16)
    if first:
        wait(got_out)
    targets = [(r.piece_a, r.base_a)]
    if len(pieces) > 1:
        targets.append((r.piece_b, r.base_b))
    for n, b in enumerate(down_blocks):
        cols = pl.ds(b, BLOCK)
        summed = dot(r.att[...], r.w_out[:, cols])
        if first:
            wait(got_down[n])
        r.sums[:, cols] = (summed + dot(r.act[...], r.w_down[:, cols])).astype(BF16)
        start = 0
        for piece, (target, base) in zip(pieces, targets):
            size = len(piece) * DRAFT
            span = pl.ds(start, size)
            writes.append(copies.start(r.sums.at[span, cols], target.at[:, cols]))
            for i in range(len(piece)):
                rows_i = pl.ds(start + i * DRAFT, DRAFT)
                kept = r.h[rows_of[start // DRAFT + i], :, cols].astype(F32) + r.bias[:, cols]
                if add_own:
                    kept = kept + r.sums[rows_i, cols].astype(F32)
                r.base[rows_i, cols] = kept
            writes.append(copies.start(r.base.at[span, cols], base.at[:, cols]))
            start += size
    wait(*writes)


def call(kernel, ins, outs, scratch, aliases, name):
    names = (*ins, *outs, *scratch)
    operands = []
    for array, space in ins.values():
        operands.append(array if space is pl.ANY else pltpu.with_memory_space_constraint(array, space))
    results = pl.pallas_call(
        functools.partial(kernel, names),
        out_shape=list(outs.values()),
        in_specs=[pl.BlockSpec(memory_space=space) for _, space in ins.values()],
        out_specs=[pl.BlockSpec(memory_space=ref.memory_space) for ref in outs.values()],
        scratch_shapes=list(scratch.values()),
        input_output_aliases={list(ins).index(a): list(outs).index(b) for a, b in aliases.items()},
        compiler_params=pltpu.CompilerParams(vmem_limit_bytes=VMEM_MIB * 2**20),
        name=name,
    )(*operands)
    return SimpleNamespace(**dict(zip(outs, results)))


def at(space, **arrays):
    return {key: (array, space) for key, array in arrays.items()}


def branch(pieces, tail, a, before):
    requests, _, width = a.hidden.shape
    heads_width = a.qkv_weight.shape[2]
    units = a.up_weight.shape[1]
    cap_len = a.key_cache.shape[1]
    acc_count = a.accepted.shape[1]
    tails = a.split_slot.shape[0]
    count = sum(len(piece) for piece in pieces)
    rows = count * DRAFT
    ins = at(
        HBM,
        lengths=a.lengths,
        split_slot=a.split_slot,
        tail_len=a.tail_len,
        accepted=a.accepted,
        parents=a.parents,
        ln_gain=a.ln_gain,
        ln_shift=a.ln_shift,
        qkv_bias=a.qkv_bias,
        up_bias=a.up_bias,
        branch_bias=a.branch_bias,
        hidden=a.hidden,
        key_cache=a.key_cache,
        value_cache=a.value_cache,
    )
    scratch = dict(
        slots=SMEM(a.split_slot.shape, I32),
        own_len=SMEM(a.lengths.shape, I32),
        all_len=SMEM(a.tail_len.shape, I32),
        tree=VMEM(a.parents.shape, I32),
        taken=VMEM(a.accepted.shape, I32),
        gain=VMEM((1, width), F32),
        shift=VMEM((1, width), F32),
        b_qkv=VMEM((3, heads_width), F32),
        b_up=VMEM((1, units), F32),
        bias=VMEM((1, width), F32),
        h=VMEM((count + (0 if tail else tails), DRAFT, width), BF16),
        normed=VMEM((rows, width), BF16),
        k_own=VMEM((count, cap_len, heads_width), BF16),
        v_own=VMEM((count, cap_len, heads_width), BF16),
        q=VMEM((rows, heads_width), BF16),
        k=VMEM((rows, heads_width), BF16),
        v=VMEM((rows, heads_width), BF16),
        att=VMEM((rows, heads_width), BF16),
        act=VMEM((rows, units), BF16),
        sums=VMEM((rows, width), BF16),
        base=VMEM((rows, width), F32),
        picked=VMEM((2, count, acc_count, heads_width), BF16),
        sems=pltpu.SemaphoreType.DMA((100,)),
    )
    outs = dict(rows_out=HBM((2, requests, acc_count, heads_width), BF16))
    aliases = {}
    if before is None:
        ins.update(
            at(
                HBM,
                qkv_weight=a.qkv_weight,
                up_weight=a.up_weight,
                down_weight=a.down_weight,
                out_weight=a.out_weight,
            )
        )
        outs.update(
            w_qkv=VMEM(a.qkv_weight.shape, BF16),
            w_up=VMEM(a.up_weight.shape, BF16),
            w_down=VMEM(a.down_weight.shape, BF16),
            w_out=VMEM(a.out_weight.shape, BF16),
        )
    else:
        ins.update(at(HBM, rows_in=before.rows_out))
        ins.update(at(VMEM, w_qkv=a.w_qkv, w_up=a.w_up, w_down=a.w_down, w_out=a.w_out))
        aliases = dict(rows_in="rows_out")
    if tail:
        ins.update(at(pl.ANY, far_keys=a.far_keys, far_values=a.far_values))
        scratch.update(k_far=VMEM(a.far_keys.shape, BF16), v_far=VMEM(a.far_values.shape, BF16))
    sizes = [len(piece) * DRAFT for piece in pieces]
    outs.update(piece_a=HBM((sizes[0], width), BF16), base_a=HBM((sizes[0], width), F32))
    if len(sizes) > 1:
        outs.update(piece_b=HBM((sizes[1], width), BF16), base_b=HBM((sizes[1], width), F32))

    def kernel(names, *refs):
        branch_kernel(pieces, before is None, a.n_mp == 2, names, *refs)

    out = call(kernel, ins, outs, scratch, aliases, "branch")
    parts = [(out.piece_a, out.base_a)]
    if len(sizes) > 1:
        parts.append((out.piece_b, out.base_b))
    if before is None:
        a.w_qkv, a.w_up, a.w_down, a.w_out = out.w_qkv, out.w_up, out.w_down, out.w_out
    return parts, out


def finish_kernel(pieces, first, names, *refs):
    r = SimpleNamespace(**{str(name): ref for name, ref in zip(names, refs)})
    given = refs[: len(pieces)]
    kept = refs[len(pieces) : 2 * len(pieces)]
    requests = r.next_qkv.shape[1]
    share = r.new_hidden.shape[0]
    places = [place for piece in pieces for place in piece]
    count = len(places)
    copies = Copies(r.sems)
    got_slots = copies.start(r.split_slot, r.slots)
    got_w = [copies.start(r.next_weight.at[c], r.w_next.at[c]) for c in range(3)] if first else []
    gain = r.next_gain[...]
    shift = r.next_shift[...]
    start = 0
    for n, piece in enumerate(pieces):
        size = len(piece) * DRAFT

        def body(k, carry, n=n, start=start):
            part = pl.ds(pl.multiple_of(k * STEP, STEP), STEP)
            rows = pl.ds(pl.multiple_of(start + k * STEP, STEP), STEP)
            new = (kept[n][part, :] + given[n][part, :].astype(F32)).astype(BF16)
            r.h[rows, :] = new
            r.normed[rows, :] = layer_norm(new.astype(F32), gain, shift).astype(BF16)
            return carry

        lax.fori_loop(0, size // STEP, body, 0, unroll=4)
        start += size

    wait(got_slots)
    order = [request_at(place, r.slots, requests) for place in places]
    rank = lax.axis_index("mp")
    new_writes = []
    for i in range(count):
        copy = copies.make(r.h.at[pl.ds(i * DRAFT, DRAFT)], r.new_hidden.at[order[i] % share])
        owned = order[i] // share == rank
        new_writes.append((owned, copy))
        pl.when(owned)(copy.start)
    writes = []
    for c in range(3):
        wait(*got_w[c : c + 1])
        linear = (dot(r.normed[...], r.w_next[c]) + r.next_bias[pl.ds(c, 1), :]).astype(BF16)
        for i in range(count):
            r.o[c, i] = linear[i * DRAFT : (i + 1) * DRAFT]
            writes.append(copies.start(r.o.at[c, i], r.next_qkv.at[c, order[i]]))
    wait(*writes)
    for owned, copy in new_writes:
        pl.when(owned)(copy.wait)


def finish(sent, a, last):
    requests, _, width = a.hidden.shape
    heads_width = a.next_weight.shape[2]
    share = requests // a.n_mp
    pieces = [piece for piece, _, _ in sent]
    count = sum(len(piece) for piece in pieces)
    rows = count * DRAFT
    ins = {}
    for _, given, _ in sent:
        ins[len(ins)] = (given, VMEM)
    for _, _, base in sent:
        ins[len(ins)] = (base, VMEM)
    ins.update(at(HBM, split_slot=a.split_slot))
    ins.update(at(VMEM, next_gain=a.next_gain, next_shift=a.next_shift, next_bias=a.next_bias))
    aliases = {}
    kept = {}
    if last is None:
        ins.update(at(HBM, next_weight=a.next_weight))
        kept = dict(w_next=VMEM(a.next_weight.shape, BF16))
    else:
        ins.update(at(VMEM, w_next=a.w_next))
        ins.update(at(HBM, new_in=last.new_hidden, qkv_in=last.next_qkv))
        aliases = dict(new_in="new_hidden", qkv_in="next_qkv")
    outs = dict(
        new_hidden=HBM((share, DRAFT, width), BF16),
        next_qkv=HBM((3, requests, DRAFT, heads_width), BF16),
        **kept,
    )
    scratch = dict(
        slots=SMEM(a.split_slot.shape, I32),
        h=VMEM((rows, width), BF16),
        normed=VMEM((rows, width), BF16),
        o=VMEM((3, count, DRAFT, heads_width), BF16),
        sems=pltpu.SemaphoreType.DMA((60,)),
    )

    def kernel(names, *refs):
        finish_kernel(pieces, last is None, names, *refs)

    out = call(kernel, ins, outs, scratch, aliases, "finish")
    if last is None:
        a.w_next = out.w_next
    return out


def local(
    hidden,
    ln_gain,
    ln_shift,
    qkv_weight,
    qkv_bias,
    out_weight,
    up_weight,
    up_bias,
    down_weight,
    branch_bias,
    next_gain,
    next_shift,
    next_weight,
    next_bias,
    key_cache,
    value_cache,
    tail_keys,
    tail_values,
    lengths,
    split_slot,
    tail_len,
    parents,
    accepted,
):
    requests = lengths.shape[0]
    width = hidden.shape[1]
    n_mp = lax.axis_size("mp")
    groups = lax.axis_size("group")
    a = SimpleNamespace(
        hidden=hidden.reshape(requests, DRAFT, width),
        ln_gain=ln_gain.reshape(1, width),
        ln_shift=ln_shift.reshape(1, width),
        qkv_weight=qkv_weight,
        qkv_bias=qkv_bias,
        out_weight=out_weight,
        up_weight=up_weight,
        up_bias=up_bias.reshape(1, -1),
        down_weight=down_weight,
        branch_bias=branch_bias.reshape(1, width),
        next_gain=next_gain.reshape(1, width),
        next_shift=next_shift.reshape(1, width),
        next_weight=next_weight,
        next_bias=next_bias,
        key_cache=key_cache,
        value_cache=value_cache,
        lengths=lengths,
        split_slot=split_slot,
        tail_len=tail_len,
        parents=parents.reshape(requests * DRAFT // PAIR, PAIR),
        accepted=accepted,
        n_mp=n_mp,
    )
    out = None
    sent = []
    for k, pieces in enumerate(CHUNKS):
        if k == 1:
            tail_keys, tail_values, _ = lax.optimization_barrier((tail_keys, tail_values, sent[0][2]))
            swap = [(i, i ^ 1) for i in range(groups)]
            a.far_keys, a.far_values = lax.ppermute((tail_keys, tail_values), "group", swap)
        if k >= 2:
            a.lengths, _ = lax.optimization_barrier((a.lengths, sent[k - 2][1]))
        sums, out = branch(pieces, k == len(CHUNKS) - 1, a, out)
        for piece, (part, kept) in zip(pieces, sums):
            if n_mp == 2:
                sent.append((piece, lax.ppermute(part, "mp", [(0, 1), (1, 0)]), kept))
            else:
                sent.append((piece, lax.psum(part, "mp"), kept))
    last = None
    for first, end in FINISHES:
        last = finish(sent[first:end], a, last)
    heads_width = qkv_weight.shape[2]
    return (
        last.new_hidden.reshape(-1, width),
        last.next_qkv.reshape(3, requests * DRAFT, heads_width),
        out.rows_out.reshape(2, -1, heads_width),
    )


def solution(mesh):
    in_specs = (
        P("group", None),
        P(),
        P(),
        P(None, None, "mp"),
        P(None, "mp"),
        P("mp", None),
        P(None, "mp"),
        P("mp"),
        P("mp", None),
        P(),
        P(),
        P(),
        P(None, None, "mp"),
        P(None, "mp"),
        P("group", None, "mp"),
        P("group", None, "mp"),
        P("group", None, "mp"),
        P("group", None, "mp"),
        P("group"),
        P("group"),
        P(),
        P("group"),
        P("group", None),
    )
    out_specs = (P(("group", "mp"), None), P(None, "group", "mp"), P(None, "group", "mp"))
    return jax.shard_map(local, mesh=mesh, in_specs=in_specs, out_specs=out_specs, check_vma=False)
```

```python
import functools
from types import SimpleNamespace

import jax
import jax.numpy as jnp
import numpy as np
from jax import lax
from jax.experimental import pallas as pl
from jax.experimental.pallas import tpu as pltpu
from jax.sharding import PartitionSpec as P

HD = 64
ROT = 32
DRAFT = 64
PAIR = 128
BLOCK = 512
STEP = 16
VMEM_MIB = 35

epsilon = 1e-05
very_low = -1e30

HBM = pltpu.HBM
VMEM = pltpu.VMEM
SMEM = pltpu.SMEM
I32 = jnp.int32
F32 = jnp.float32
BF16 = jnp.bfloat16

CHUNKS = (((0, 1),), ((2, 3, 4),), ((5, 6),), ((7,),))
FINISHES = ((0, 2), (2, 3), (3, 4))


def dot(a, b):
    return jnp.dot(a, b, preferred_element_type=F32)


def dot_nt(a, b):
    return lax.dot_general(a, b, (((1,), (1,)), ((), ())), preferred_element_type=F32)


def request_at(place, slots, requests):
    tails = slots.shape[0]
    whole = requests - tails
    if place >= whole:
        return slots[place - whole]
    ordered = [slots[t] for t in range(tails)]
    for end in range(tails - 1, 0, -1):
        for t in range(end):
            low = jnp.minimum(ordered[t], ordered[t + 1])
            high = jnp.maximum(ordered[t], ordered[t + 1])
            ordered[t], ordered[t + 1] = low, high
    request = jnp.int32(place)
    for slot in ordered:
        request = request + (request >= slot).astype(I32)
    return request


class Copies:
    def __init__(self, sems):
        self.sems = sems
        self.used = 0

    def make(self, source, target):
        copy = pltpu.make_async_copy(source, target, self.sems.at[self.used])
        self.used += 1
        return copy

    def start(self, source, target):
        copy = self.make(source, target)
        copy.start()
        return copy


def wait(*copies):
    for copy in copies:
        copy.wait()


def layer_norm(values, gain, shift):
    centred = values - jnp.mean(values, axis=-1, keepdims=True)
    variance = jnp.mean(centred * centred, axis=-1, keepdims=True)
    return centred * lax.rsqrt(variance + epsilon) * gain + shift


def ancestor_pair(parents, first, second):
    lane = lax.broadcasted_iota(I32, (1, PAIR), 1)

    def row_of(request, half):
        row = parents[pl.ds(request // 2, 1), :]
        return jnp.where(request % 2 == half, row, pltpu.roll(row, DRAFT, 1))

    ids = jnp.where(lane < DRAFT, row_of(first, 0), row_of(second, 1) + DRAFT)
    row_id = lax.broadcasted_iota(I32, (PAIR, PAIR), 0)
    col_id = lax.broadcasted_iota(I32, (PAIR, PAIR), 1)
    below = jnp.where(row_id == ids, 1.0, 0.0).astype(BF16)
    same = jnp.where(row_id == col_id, 1.0, 0.0).astype(BF16)
    reach = jnp.minimum(dot_nt(same, below) + same.astype(F32), 1.0)
    for _ in range((DRAFT - 1).bit_length()):
        half = reach.astype(BF16)
        reach = jnp.minimum(dot(half, half), 1.0)
    return reach


def rotary_tables(positions):
    feature = lax.broadcasted_iota(I32, (1, PAIR), 1) % HD
    inverse = jnp.zeros((1, PAIR), F32)
    for k in range(ROT // 2):
        rate = float(np.float32(10000.0 ** (-k * 2.0 / ROT)))
        inverse = jnp.where(feature % (ROT // 2) == k, rate, inverse)
    angles = positions * inverse
    sine = jnp.sin(angles)
    same = jnp.where(feature < ROT, jnp.cos(angles), 1.0)
    ahead = jnp.where(feature < ROT // 2, -sine, 0.0)
    behind = jnp.where((feature >= ROT // 2) & (feature < ROT), sine, 0.0)
    return same, ahead, behind


def rotate(values, tables):
    same, ahead, behind = tables
    half_rot = ROT // 2
    parts = []
    for start in range(0, values.shape[1], PAIR):
        part = values[:, start : start + PAIR]
        parts.append(
            part * same
            + pltpu.roll(part, PAIR - half_rot, 1) * ahead
            + pltpu.roll(part, half_rot, 1) * behind
        )
    return jnp.concatenate(parts, axis=1) if len(parts) > 1 else parts[0]


def gelu(v):
    inner = np.float32(np.sqrt(2.0 / np.pi)) * (v + 0.044715 * (v * v * v))
    return 0.5 * v * (1.0 + jnp.tanh(inner))


def picks(accepted, request, tokens):
    count = accepted.shape[1]
    row = accepted[pl.ds(request, 1), :]
    row_id = lax.broadcasted_iota(I32, (count, count), 0)
    col_id = lax.broadcasted_iota(I32, (count, count), 1)
    ids = jnp.sum(jnp.where(row_id == col_id, row, 0).astype(F32), axis=1, keepdims=True)
    token_id = lax.broadcasted_iota(I32, (count, tokens), 1).astype(F32)
    return jnp.where(token_id == ids, 1.0, 0.0).astype(BF16)


def branch_kernel(pieces, first, add_own, names, *refs):
    r = SimpleNamespace(**dict(zip(names, refs)))
    places = [place for piece in pieces for place in piece]
    count = len(places)
    rows = count * DRAFT
    requests, _, width = r.hidden.shape
    heads_width = r.w_qkv.shape[2]
    units = r.w_up.shape[1]
    cap_len = r.key_cache.shape[1]
    tails = r.split_slot.shape[0]
    whole = requests - tails
    group = min(heads_width, 4 * HD)
    per = group // HD
    copies = Copies(r.sems)

    got_scalars = [
        copies.start(r.split_slot, r.slots),
        copies.start(r.lengths, r.own_len),
        copies.start(r.tail_len, r.all_len),
    ]
    got_small = [
        copies.start(r.parents, r.tree),
        copies.start(r.accepted, r.taken),
        copies.start(r.ln_gain, r.gain),
        copies.start(r.ln_shift, r.shift),
        copies.start(r.qkv_bias, r.b_qkv),
        copies.start(r.up_bias, r.b_up),
        copies.start(r.branch_bias, r.bias),
    ]
    early = places[-1] < whole
    if early:
        span = pl.ds(places[0], places[-1] - places[0] + 1 + tails)
        got_hidden = [copies.start(r.hidden.at[span], r.h)]
    got_qkv = [copies.start(r.qkv_weight.at[c], r.w_qkv.at[c]) for c in range(3)] if first else []
    wait(*got_scalars)
    order = [request_at(place, r.slots, requests) for place in places]
    far_base = jnp.bitwise_xor(lax.axis_index("group"), 1) * tails
    if not early:
        got_hidden = [copies.start(r.hidden.at[order[i]], r.h.at[i]) for i in range(count)]
        rows_of = range(count)
    else:
        rows_of = [request - places[0] for request in order]
    got_own = [
        (
            copies.start(r.key_cache.at[order[i]], r.k_own.at[i]),
            copies.start(r.value_cache.at[order[i]], r.v_own.at[i]),
        )
        for i in range(count)
    ]
    up_blocks = range(0, units, BLOCK)
    down_blocks = range(0, width, BLOCK)
    if first:
        got_up = [
            copies.start(r.up_weight.at[:, pl.ds(b, BLOCK)], r.w_up.at[:, pl.ds(b, BLOCK)])
            for b in up_blocks
        ]
        got_out = copies.start(r.out_weight, r.w_out)
        got_down = [
            copies.start(r.down_weight.at[:, pl.ds(b, BLOCK)], r.w_down.at[:, pl.ds(b, BLOCK)])
            for b in down_blocks
        ]
    if places[-1] >= whole:
        held = [place - whole for place in places if place >= whole]
        got_far = [
            (copies.start(r.far_keys.at[t], r.k_far.at[n]), copies.start(r.far_values.at[t], r.v_far.at[n]))
            for n, t in enumerate(held)
        ]

    wait(*got_small)
    reach = []
    tables = []
    for i in range(0, count, 2):
        both = ancestor_pair(r.tree, order[i], order[min(i + 1, count - 1)])
        depth = jnp.sum(both, axis=1, keepdims=True) - 1.0
        for k in range(min(2, count - i)):
            span = slice(k * DRAFT, (k + 1) * DRAFT)
            reach.append(both[span, span])
            base = r.own_len[order[i + k]].astype(F32)
            if places[i + k] >= whole:
                base = base + r.all_len[far_base + places[i + k] - whole].astype(F32)
            tables.append(rotary_tables(base + depth[span]))

    wait(*got_hidden)
    gain = r.gain[...]
    shift = r.shift[...]

    for i in range(count):
        for k in range(0, DRAFT, STEP):
            values = r.h[rows_of[i], pl.ds(k, STEP), :].astype(F32)
            r.normed[pl.ds(i * DRAFT + k, STEP), :] = layer_norm(values, gain, shift).astype(BF16)

    for c, target in enumerate((r.q, r.k, r.v)):
        wait(*got_qkv[c : c + 1])
        linear = dot(r.normed[...], r.w_qkv[c]) + r.b_qkv[pl.ds(c, 1), :]
        for i in range(count):
            part = linear[i * DRAFT : (i + 1) * DRAFT]
            if c < 2:
                part = rotate(part, tables[i])
            part = part.astype(BF16)
            if c == 0:
                part = part * np.float32(HD**-0.5).astype(BF16)
            target[pl.ds(i * DRAFT, DRAFT), :] = part

    writes = []
    for i in range(count):
        hot = picks(r.taken, order[i], DRAFT)
        for c, source in enumerate((r.k, r.v)):
            r.picked[c, i] = dot(hot, source[pl.ds(i * DRAFT, DRAFT), :]).astype(BF16)
            writes.append(copies.start(r.picked.at[c, i], r.rows_out.at[c, order[i]]))

    lane_head = lax.broadcasted_iota(I32, (DRAFT, group), 1) // HD
    for i in range(count):
        wait(*got_own[i])
        t = places[i] - whole
        if t >= 0:
            n_far = held.index(t)
            wait(*got_far[n_far])
        span = pl.ds(i * DRAFT, DRAFT)
        key_id = lax.broadcasted_iota(I32, (1, cap_len), 1)
        own_bias = jnp.where(key_id < r.own_len[order[i]], 0.0, very_low)
        tree_bias = jnp.where(reach[i] > 0.5, 0.0, very_low)
        tree_bias = jnp.concatenate([tree_bias] * per, axis=0)
        for low in range(0, heads_width, group):
            cols = slice(low, low + group)
            query = r.q[span, cols]
            query = jnp.concatenate(
                [jnp.where(lane_head == h, query, jnp.zeros_like(query)) for h in range(per)], axis=0
            )
            own = dot_nt(query, r.k_own[i, :, cols]) + own_bias
            tree = dot_nt(query, r.k[span, cols]) + tree_bias
            top = jnp.maximum(
                jnp.max(own, axis=1, keepdims=True), jnp.max(tree, axis=1, keepdims=True)
            )
            own = jnp.exp(own - top)
            tree = jnp.exp(tree - top)
            total = jnp.sum(own, axis=1, keepdims=True) + jnp.sum(tree, axis=1, keepdims=True)
            mixed = dot(own.astype(BF16), r.v_own[i, :, cols])
            mixed = mixed + dot(tree.astype(BF16), r.v[span, cols])
            if t >= 0:
                far_cap = r.k_far.shape[1]
                far_len = r.all_len[far_base + t]
                for start in range(0, far_cap, BLOCK):
                    part = slice(start, start + BLOCK)
                    far_id = lax.broadcasted_iota(I32, (1, BLOCK), 1) + start
                    far_bias = jnp.where(far_id < far_len, 0.0, very_low)
                    far = dot_nt(query, r.k_far[n_far, part, cols]) + far_bias
                    peak = jnp.maximum(top, jnp.max(far, axis=1, keepdims=True))
                    keep = jnp.exp(top - peak)
                    far = jnp.exp(far - peak)
                    total = total * keep + jnp.sum(far, axis=1, keepdims=True)
                    mixed = mixed * keep + dot(far.astype(BF16), r.v_far[n_far, part, cols])
                    top = peak
            mixed = mixed * (1.0 / total)
            joined = jnp.zeros((DRAFT, group), F32)
            for h in range(per):
                joined = jnp.where(lane_head == h, mixed[h * DRAFT : (h + 1) * DRAFT], joined)
            r.att[span, cols] = joined.astype(BF16)

    for n, b in enumerate(up_blocks):
        if first:
            wait(got_up[n])
        cols = pl.ds(b, BLOCK)
        r.act[:, cols] = gelu(dot(r.normed[...], r.w_up[:, cols]) + r.b_up[:, cols]).astype(BF16)
    if first:
        wait(got_out)
    targets = [(r.piece_a, r.base_a)]
    if len(pieces) > 1:
        targets.append((r.piece_b, r.base_b))
    for n, b in enumerate(down_blocks):
        cols = pl.ds(b, BLOCK)
        summed = dot(r.att[...], r.w_out[:, cols])
        if first:
            wait(got_down[n])
        r.sums[:, cols] = (summed + dot(r.act[...], r.w_down[:, cols])).astype(BF16)
        start = 0
        for piece, (target, base) in zip(pieces, targets):
            size = len(piece) * DRAFT
            span = pl.ds(start, size)
            writes.append(copies.start(r.sums.at[span, cols], target.at[:, cols]))
            for i in range(len(piece)):
                rows_i = pl.ds(start + i * DRAFT, DRAFT)
                kept = r.h[rows_of[start // DRAFT + i], :, cols].astype(F32) + r.bias[:, cols]
                if add_own:
                    kept = kept + r.sums[rows_i, cols].astype(F32)
                r.base[rows_i, cols] = kept
            writes.append(copies.start(r.base.at[span, cols], base.at[:, cols]))
            start += size
    wait(*writes)


def call(kernel, ins, outs, scratch, aliases, name):
    names = (*ins, *outs, *scratch)
    operands = []
    for array, space in ins.values():
        operands.append(array if space is pl.ANY else pltpu.with_memory_space_constraint(array, space))
    results = pl.pallas_call(
        functools.partial(kernel, names),
        out_shape=list(outs.values()),
        in_specs=[pl.BlockSpec(memory_space=space) for _, space in ins.values()],
        out_specs=[pl.BlockSpec(memory_space=ref.memory_space) for ref in outs.values()],
        scratch_shapes=list(scratch.values()),
        input_output_aliases={list(ins).index(a): list(outs).index(b) for a, b in aliases.items()},
        compiler_params=pltpu.CompilerParams(vmem_limit_bytes=VMEM_MIB * 2**20),
        name=name,
    )(*operands)
    return SimpleNamespace(**dict(zip(outs, results)))


def at(space, **arrays):
    return {key: (array, space) for key, array in arrays.items()}


def branch(pieces, a, before):
    requests, _, width = a.hidden.shape
    heads_width = a.qkv_weight.shape[2]
    units = a.up_weight.shape[1]
    cap_len = a.key_cache.shape[1]
    acc_count = a.accepted.shape[1]
    tails = a.split_slot.shape[0]
    count = sum(len(piece) for piece in pieces)
    rows = count * DRAFT
    tail = sum(place >= requests - tails for piece in pieces for place in piece)
    ins = at(
        HBM,
        lengths=a.lengths,
        split_slot=a.split_slot,
        tail_len=a.tail_len,
        accepted=a.accepted,
        parents=a.parents,
        ln_gain=a.ln_gain,
        ln_shift=a.ln_shift,
        qkv_bias=a.qkv_bias,
        up_bias=a.up_bias,
        branch_bias=a.branch_bias,
        hidden=a.hidden,
        key_cache=a.key_cache,
        value_cache=a.value_cache,
    )
    scratch = dict(
        slots=SMEM(a.split_slot.shape, I32),
        own_len=SMEM(a.lengths.shape, I32),
        all_len=SMEM(a.tail_len.shape, I32),
        tree=VMEM(a.parents.shape, I32),
        taken=VMEM(a.accepted.shape, I32),
        gain=VMEM((1, width), F32),
        shift=VMEM((1, width), F32),
        b_qkv=VMEM((3, heads_width), F32),
        b_up=VMEM((1, units), F32),
        bias=VMEM((1, width), F32),
        h=VMEM((count + (0 if tail else tails), DRAFT, width), BF16),
        normed=VMEM((rows, width), BF16),
        k_own=VMEM((count, cap_len, heads_width), BF16),
        v_own=VMEM((count, cap_len, heads_width), BF16),
        q=VMEM((rows, heads_width), BF16),
        k=VMEM((rows, heads_width), BF16),
        v=VMEM((rows, heads_width), BF16),
        att=VMEM((rows, heads_width), BF16),
        act=VMEM((rows, units), BF16),
        sums=VMEM((rows, width), BF16),
        base=VMEM((rows, width), F32),
        picked=VMEM((2, count, acc_count, heads_width), BF16),
        sems=pltpu.SemaphoreType.DMA((100,)),
    )
    outs = dict(rows_out=HBM((2, requests, acc_count, heads_width), BF16))
    aliases = {}
    if before is None:
        ins.update(
            at(
                HBM,
                qkv_weight=a.qkv_weight,
                up_weight=a.up_weight,
                down_weight=a.down_weight,
                out_weight=a.out_weight,
            )
        )
        outs.update(
            w_qkv=VMEM(a.qkv_weight.shape, BF16),
            w_up=VMEM(a.up_weight.shape, BF16),
            w_down=VMEM(a.down_weight.shape, BF16),
            w_out=VMEM(a.out_weight.shape, BF16),
        )
    else:
        ins.update(at(HBM, rows_in=before.rows_out))
        ins.update(at(VMEM, w_qkv=a.w_qkv, w_up=a.w_up, w_down=a.w_down, w_out=a.w_out))
        aliases = dict(rows_in="rows_out")
    if tail:
        ins.update(at(pl.ANY, far_keys=a.far_keys, far_values=a.far_values))
        far_shape = (tail, *a.far_keys.shape[1:])
        scratch.update(k_far=VMEM(far_shape, BF16), v_far=VMEM(far_shape, BF16))
    sizes = [len(piece) * DRAFT for piece in pieces]
    outs.update(piece_a=HBM((sizes[0], width), BF16), base_a=HBM((sizes[0], width), F32))
    if len(sizes) > 1:
        outs.update(piece_b=HBM((sizes[1], width), BF16), base_b=HBM((sizes[1], width), F32))

    def kernel(names, *refs):
        branch_kernel(pieces, before is None, a.n_mp == 2, names, *refs)

    out = call(kernel, ins, outs, scratch, aliases, "branch")
    parts = [(out.piece_a, out.base_a)]
    if len(sizes) > 1:
        parts.append((out.piece_b, out.base_b))
    if before is None:
        a.w_qkv, a.w_up, a.w_down, a.w_out = out.w_qkv, out.w_up, out.w_down, out.w_out
    return parts, out


def finish_kernel(pieces, first, names, *refs):
    r = SimpleNamespace(**{str(name): ref for name, ref in zip(names, refs)})
    given = refs[: len(pieces)]
    kept = refs[len(pieces) : 2 * len(pieces)]
    requests = r.next_qkv.shape[1]
    share = r.new_hidden.shape[0]
    places = [place for piece in pieces for place in piece]
    count = len(places)
    copies = Copies(r.sems)
    got_slots = copies.start(r.split_slot, r.slots)
    got_w = [copies.start(r.next_weight.at[c], r.w_next.at[c]) for c in range(3)] if first else []
    gain = r.next_gain[...]
    shift = r.next_shift[...]
    start = 0
    for n, piece in enumerate(pieces):
        size = len(piece) * DRAFT

        def body(k, carry, n=n, start=start):
            part = pl.ds(pl.multiple_of(k * STEP, STEP), STEP)
            rows = pl.ds(pl.multiple_of(start + k * STEP, STEP), STEP)
            new = (kept[n][part, :] + given[n][part, :].astype(F32)).astype(BF16)
            r.h[rows, :] = new
            r.normed[rows, :] = layer_norm(new.astype(F32), gain, shift).astype(BF16)
            return carry

        lax.fori_loop(0, size // STEP, body, 0, unroll=4)
        start += size

    wait(got_slots)
    order = [request_at(place, r.slots, requests) for place in places]
    rank = lax.axis_index("mp")
    new_writes = []
    for i in range(count):
        copy = copies.make(r.h.at[pl.ds(i * DRAFT, DRAFT)], r.new_hidden.at[order[i] % share])
        owned = order[i] // share == rank
        new_writes.append((owned, copy))
        pl.when(owned)(copy.start)
    writes = []
    for c in range(3):
        wait(*got_w[c : c + 1])
        linear = (dot(r.normed[...], r.w_next[c]) + r.next_bias[pl.ds(c, 1), :]).astype(BF16)
        for i in range(count):
            r.o[c, i] = linear[i * DRAFT : (i + 1) * DRAFT]
            writes.append(copies.start(r.o.at[c, i], r.next_qkv.at[c, order[i]]))
    wait(*writes)
    for owned, copy in new_writes:
        pl.when(owned)(copy.wait)


def finish(sent, a, last):
    requests, _, width = a.hidden.shape
    heads_width = a.next_weight.shape[2]
    share = requests // a.n_mp
    pieces = [piece for piece, _, _ in sent]
    count = sum(len(piece) for piece in pieces)
    rows = count * DRAFT
    ins = {}
    for _, given, _ in sent:
        ins[len(ins)] = (given, VMEM)
    for _, _, base in sent:
        ins[len(ins)] = (base, VMEM)
    ins.update(at(HBM, split_slot=a.split_slot))
    ins.update(at(VMEM, next_gain=a.next_gain, next_shift=a.next_shift, next_bias=a.next_bias))
    aliases = {}
    kept = {}
    if last is None:
        ins.update(at(HBM, next_weight=a.next_weight))
        kept = dict(w_next=VMEM(a.next_weight.shape, BF16))
    else:
        ins.update(at(VMEM, w_next=a.w_next))
        ins.update(at(HBM, new_in=last.new_hidden, qkv_in=last.next_qkv))
        aliases = dict(new_in="new_hidden", qkv_in="next_qkv")
    outs = dict(
        new_hidden=HBM((share, DRAFT, width), BF16),
        next_qkv=HBM((3, requests, DRAFT, heads_width), BF16),
        **kept,
    )
    scratch = dict(
        slots=SMEM(a.split_slot.shape, I32),
        h=VMEM((rows, width), BF16),
        normed=VMEM((rows, width), BF16),
        o=VMEM((3, count, DRAFT, heads_width), BF16),
        sems=pltpu.SemaphoreType.DMA((60,)),
    )

    def kernel(names, *refs):
        finish_kernel(pieces, last is None, names, *refs)

    out = call(kernel, ins, outs, scratch, aliases, "finish")
    if last is None:
        a.w_next = out.w_next
    return out


def local(
    hidden,
    ln_gain,
    ln_shift,
    qkv_weight,
    qkv_bias,
    out_weight,
    up_weight,
    up_bias,
    down_weight,
    branch_bias,
    next_gain,
    next_shift,
    next_weight,
    next_bias,
    key_cache,
    value_cache,
    tail_keys,
    tail_values,
    lengths,
    split_slot,
    tail_len,
    parents,
    accepted,
):
    requests = lengths.shape[0]
    width = hidden.shape[1]
    n_mp = lax.axis_size("mp")
    groups = lax.axis_size("group")
    a = SimpleNamespace(
        hidden=hidden.reshape(requests, DRAFT, width),
        ln_gain=ln_gain.reshape(1, width),
        ln_shift=ln_shift.reshape(1, width),
        qkv_weight=qkv_weight,
        qkv_bias=qkv_bias,
        out_weight=out_weight,
        up_weight=up_weight,
        up_bias=up_bias.reshape(1, -1),
        down_weight=down_weight,
        branch_bias=branch_bias.reshape(1, width),
        next_gain=next_gain.reshape(1, width),
        next_shift=next_shift.reshape(1, width),
        next_weight=next_weight,
        next_bias=next_bias,
        key_cache=key_cache,
        value_cache=value_cache,
        lengths=lengths,
        split_slot=split_slot,
        tail_len=tail_len,
        parents=parents.reshape(requests * DRAFT // PAIR, PAIR),
        accepted=accepted,
        n_mp=n_mp,
    )
    out = None
    sent = []
    for k, pieces in enumerate(CHUNKS):
        if k == 1:
            tail_keys, tail_values, _ = lax.optimization_barrier((tail_keys, tail_values, sent[0][2]))
            swap = [(i, i ^ 1) for i in range(groups)]
            a.far_keys, a.far_values = lax.ppermute((tail_keys, tail_values), "group", swap)
        if k == 2:
            a.lengths, _ = lax.optimization_barrier((a.lengths, sent[k - 2][1]))
        sums, out = branch(pieces, a, out)
        for piece, (part, kept) in zip(pieces, sums):
            if n_mp == 2:
                sent.append((piece, lax.ppermute(part, "mp", [(0, 1), (1, 0)]), kept))
            else:
                sent.append((piece, lax.psum(part, "mp"), kept))
    last = None
    for first, end in FINISHES:
        last = finish(sent[first:end], a, last)
    heads_width = qkv_weight.shape[2]
    return (
        last.new_hidden.reshape(-1, width),
        last.next_qkv.reshape(3, requests * DRAFT, heads_width),
        out.rows_out.reshape(2, -1, heads_width),
    )


def solution(mesh):
    in_specs = (
        P("group", None),
        P(),
        P(),
        P(None, None, "mp"),
        P(None, "mp"),
        P("mp", None),
        P(None, "mp"),
        P("mp"),
        P("mp", None),
        P(),
        P(),
        P(),
        P(None, None, "mp"),
        P(None, "mp"),
        P("group", None, "mp"),
        P("group", None, "mp"),
        P("group", None, "mp"),
        P("group", None, "mp"),
        P("group"),
        P("group"),
        P(),
        P("group"),
        P("group", None),
    )
    out_specs = (P(("group", "mp"), None), P(None, "group", "mp"), P(None, "group", "mp"))
    return jax.shard_map(local, mesh=mesh, in_specs=in_specs, out_specs=out_specs, check_vma=False)
```

```python
import functools
from types import SimpleNamespace

import jax
import jax.numpy as jnp
import numpy as np
from jax import lax
from jax.experimental import pallas as pl
from jax.experimental.pallas import tpu as pltpu
from jax.sharding import PartitionSpec as P

HD = 64
ROT = 32
DRAFT = 64
PAIR = 128
BLOCK = 512
FAR_BLOCK = 1024
STEP = 16
VMEM_MIB = 35

epsilon = 1e-05
very_low = -1e30

HBM = pltpu.HBM
VMEM = pltpu.VMEM
SMEM = pltpu.SMEM
I32 = jnp.int32
F32 = jnp.float32
BF16 = jnp.bfloat16

CHUNKS = (((0, 1),), ((2, 3, 4),), ((5, 6),), ((7,),))
FINISHES = ((0, 2), (2, 3), (3, 4))


def dot(a, b):
    return jnp.dot(a, b, preferred_element_type=F32)


def dot_nt(a, b):
    return lax.dot_general(a, b, (((1,), (1,)), ((), ())), preferred_element_type=F32)


def request_at(place, slots, requests):
    tails = slots.shape[0]
    whole = requests - tails
    if place >= whole:
        return slots[place - whole]
    ordered = [slots[t] for t in range(tails)]
    for end in range(tails - 1, 0, -1):
        for t in range(end):
            low = jnp.minimum(ordered[t], ordered[t + 1])
            high = jnp.maximum(ordered[t], ordered[t + 1])
            ordered[t], ordered[t + 1] = low, high
    request = jnp.int32(place)
    for slot in ordered:
        request = request + (request >= slot).astype(I32)
    return request


class Copies:
    def __init__(self, sems):
        self.sems = sems
        self.used = 0

    def make(self, source, target):
        copy = pltpu.make_async_copy(source, target, self.sems.at[self.used])
        self.used += 1
        return copy

    def start(self, source, target):
        copy = self.make(source, target)
        copy.start()
        return copy


def wait(*copies):
    for copy in copies:
        copy.wait()


def layer_norm(values, gain, shift):
    centred = values - jnp.mean(values, axis=-1, keepdims=True)
    variance = jnp.mean(centred * centred, axis=-1, keepdims=True)
    return centred * lax.rsqrt(variance + epsilon) * gain + shift


def ancestor_pair(parents, first, second):
    lane = lax.broadcasted_iota(I32, (1, PAIR), 1)

    def row_of(request, half):
        row = parents[pl.ds(request // 2, 1), :]
        return jnp.where(request % 2 == half, row, pltpu.roll(row, DRAFT, 1))

    ids = jnp.where(lane < DRAFT, row_of(first, 0), row_of(second, 1) + DRAFT)
    row_id = lax.broadcasted_iota(I32, (PAIR, PAIR), 0)
    col_id = lax.broadcasted_iota(I32, (PAIR, PAIR), 1)
    below = jnp.where(row_id == ids, 1.0, 0.0).astype(BF16)
    same = jnp.where(row_id == col_id, 1.0, 0.0).astype(BF16)
    reach = jnp.minimum(dot_nt(same, below) + same.astype(F32), 1.0)
    for _ in range((DRAFT - 1).bit_length()):
        half = reach.astype(BF16)
        reach = jnp.minimum(dot(half, half), 1.0)
    return reach


def rotary_tables(positions):
    feature = lax.broadcasted_iota(I32, (1, PAIR), 1) % HD
    inverse = jnp.zeros((1, PAIR), F32)
    for k in range(ROT // 2):
        rate = float(np.float32(10000.0 ** (-k * 2.0 / ROT)))
        inverse = jnp.where(feature % (ROT // 2) == k, rate, inverse)
    angles = positions * inverse
    sine = jnp.sin(angles)
    same = jnp.where(feature < ROT, jnp.cos(angles), 1.0)
    ahead = jnp.where(feature < ROT // 2, -sine, 0.0)
    behind = jnp.where((feature >= ROT // 2) & (feature < ROT), sine, 0.0)
    return same, ahead, behind


def rotate(values, tables):
    same, ahead, behind = tables
    half_rot = ROT // 2
    parts = []
    for start in range(0, values.shape[1], PAIR):
        part = values[:, start : start + PAIR]
        parts.append(
            part * same
            + pltpu.roll(part, PAIR - half_rot, 1) * ahead
            + pltpu.roll(part, half_rot, 1) * behind
        )
    return jnp.concatenate(parts, axis=1) if len(parts) > 1 else parts[0]


def gelu(v):
    inner = np.float32(np.sqrt(2.0 / np.pi)) * (v + 0.044715 * (v * v * v))
    return 0.5 * v * (1.0 + jnp.tanh(inner))


def picks(accepted, request, tokens):
    count = accepted.shape[1]
    row = accepted[pl.ds(request, 1), :]
    row_id = lax.broadcasted_iota(I32, (count, count), 0)
    col_id = lax.broadcasted_iota(I32, (count, count), 1)
    ids = jnp.sum(jnp.where(row_id == col_id, row, 0).astype(F32), axis=1, keepdims=True)
    token_id = lax.broadcasted_iota(I32, (count, tokens), 1).astype(F32)
    return jnp.where(token_id == ids, 1.0, 0.0).astype(BF16)


def branch_kernel(pieces, first, add_own, names, *refs):
    r = SimpleNamespace(**dict(zip(names, refs)))
    places = [place for piece in pieces for place in piece]
    count = len(places)
    rows = count * DRAFT
    requests, _, width = r.hidden.shape
    heads_width = r.w_qkv.shape[2]
    units = r.w_up.shape[1]
    cap_len = r.key_cache.shape[1]
    tails = r.split_slot.shape[0]
    whole = requests - tails
    group = min(heads_width, 4 * HD)
    per = group // HD
    copies = Copies(r.sems)

    got_scalars = [
        copies.start(r.split_slot, r.slots),
        copies.start(r.lengths, r.own_len),
        copies.start(r.tail_len, r.all_len),
    ]
    got_small = [
        copies.start(r.parents, r.tree),
        copies.start(r.accepted, r.taken),
        copies.start(r.ln_gain, r.gain),
        copies.start(r.ln_shift, r.shift),
        copies.start(r.qkv_bias, r.b_qkv),
        copies.start(r.up_bias, r.b_up),
        copies.start(r.branch_bias, r.bias),
    ]
    early = places[-1] < whole
    if early:
        span = pl.ds(places[0], places[-1] - places[0] + 1 + tails)
        got_hidden = [copies.start(r.hidden.at[span], r.h)]
    got_qkv = [copies.start(r.qkv_weight.at[c], r.w_qkv.at[c]) for c in range(3)] if first else []
    wait(*got_scalars)
    order = [request_at(place, r.slots, requests) for place in places]
    far_base = jnp.bitwise_xor(lax.axis_index("group"), 1) * tails
    if not early:
        got_hidden = [copies.start(r.hidden.at[order[i]], r.h.at[i]) for i in range(count)]
        rows_of = range(count)
    else:
        rows_of = [request - places[0] for request in order]
    got_own = [
        (
            copies.start(r.key_cache.at[order[i]], r.k_own.at[i]),
            copies.start(r.value_cache.at[order[i]], r.v_own.at[i]),
        )
        for i in range(count)
    ]
    up_blocks = range(0, units, BLOCK)
    down_blocks = range(0, width, BLOCK)
    if first:
        got_up = [
            copies.start(r.up_weight.at[:, pl.ds(b, BLOCK)], r.w_up.at[:, pl.ds(b, BLOCK)])
            for b in up_blocks
        ]
        got_out = copies.start(r.out_weight, r.w_out)
        got_down = [
            copies.start(r.down_weight.at[:, pl.ds(b, BLOCK)], r.w_down.at[:, pl.ds(b, BLOCK)])
            for b in down_blocks
        ]
    if places[-1] >= whole:
        held = [place - whole for place in places if place >= whole]
        got_far = [
            (copies.start(r.far_keys.at[t], r.k_far.at[n]), copies.start(r.far_values.at[t], r.v_far.at[n]))
            for n, t in enumerate(held)
        ]

    wait(*got_small)
    reach = []
    tables = []
    for i in range(0, count, 2):
        both = ancestor_pair(r.tree, order[i], order[min(i + 1, count - 1)])
        depth = jnp.sum(both, axis=1, keepdims=True) - 1.0
        for k in range(min(2, count - i)):
            span = slice(k * DRAFT, (k + 1) * DRAFT)
            reach.append(both[span, span])
            base = r.own_len[order[i + k]].astype(F32)
            if places[i + k] >= whole:
                base = base + r.all_len[far_base + places[i + k] - whole].astype(F32)
            tables.append(rotary_tables(base + depth[span]))

    wait(*got_hidden)
    gain = r.gain[...]
    shift = r.shift[...]

    for i in range(count):
        for k in range(0, DRAFT, STEP):
            values = r.h[rows_of[i], pl.ds(k, STEP), :].astype(F32)
            r.normed[pl.ds(i * DRAFT + k, STEP), :] = layer_norm(values, gain, shift).astype(BF16)

    for c, target in enumerate((r.q, r.k, r.v)):
        wait(*got_qkv[c : c + 1])
        linear = dot(r.normed[...], r.w_qkv[c]) + r.b_qkv[pl.ds(c, 1), :]
        for i in range(count):
            part = linear[i * DRAFT : (i + 1) * DRAFT]
            if c < 2:
                part = rotate(part, tables[i])
            part = part.astype(BF16)
            if c == 0:
                part = part * np.float32(HD**-0.5).astype(BF16)
            target[pl.ds(i * DRAFT, DRAFT), :] = part

    writes = []
    for i in range(count):
        hot = picks(r.taken, order[i], DRAFT)
        for c, source in enumerate((r.k, r.v)):
            r.picked[c, i] = dot(hot, source[pl.ds(i * DRAFT, DRAFT), :]).astype(BF16)
            writes.append(copies.start(r.picked.at[c, i], r.rows_out.at[c, order[i]]))

    lane_head = lax.broadcasted_iota(I32, (DRAFT, group), 1) // HD
    for i in range(count):
        wait(*got_own[i])
        t = places[i] - whole
        if t >= 0:
            n_far = held.index(t)
            wait(*got_far[n_far])
        span = pl.ds(i * DRAFT, DRAFT)
        key_id = lax.broadcasted_iota(I32, (1, cap_len), 1)
        own_bias = jnp.where(key_id < r.own_len[order[i]], 0.0, very_low)
        tree_bias = jnp.where(reach[i] > 0.5, 0.0, very_low)
        tree_bias = jnp.concatenate([tree_bias] * per, axis=0)
        for low in range(0, heads_width, group):
            cols = slice(low, low + group)
            query = r.q[span, cols]
            query = jnp.concatenate(
                [jnp.where(lane_head == h, query, jnp.zeros_like(query)) for h in range(per)], axis=0
            )
            own = dot_nt(query, r.k_own[i, :, cols]) + own_bias
            tree = dot_nt(query, r.k[span, cols]) + tree_bias
            top = jnp.maximum(
                jnp.max(own, axis=1, keepdims=True), jnp.max(tree, axis=1, keepdims=True)
            )
            own = jnp.exp(own - top)
            tree = jnp.exp(tree - top)
            total = jnp.sum(own, axis=1, keepdims=True) + jnp.sum(tree, axis=1, keepdims=True)
            mixed = dot(own.astype(BF16), r.v_own[i, :, cols])
            mixed = mixed + dot(tree.astype(BF16), r.v[span, cols])
            if t >= 0:
                far_cap = r.k_far.shape[1]
                far_len = r.all_len[far_base + t]
                for start in range(0, far_cap, FAR_BLOCK):
                    part = slice(start, start + FAR_BLOCK)
                    far_id = lax.broadcasted_iota(I32, (1, FAR_BLOCK), 1) + start
                    far_bias = jnp.where(far_id < far_len, 0.0, very_low)
                    far = dot_nt(query, r.k_far[n_far, part, cols]) + far_bias
                    peak = jnp.maximum(top, jnp.max(far, axis=1, keepdims=True))
                    keep = jnp.exp(top - peak)
                    far = jnp.exp(far - peak)
                    total = total * keep + jnp.sum(far, axis=1, keepdims=True)
                    mixed = mixed * keep + dot(far.astype(BF16), r.v_far[n_far, part, cols])
                    top = peak
            mixed = mixed * (1.0 / total)
            joined = jnp.zeros((DRAFT, group), F32)
            for h in range(per):
                joined = jnp.where(lane_head == h, mixed[h * DRAFT : (h + 1) * DRAFT], joined)
            r.att[span, cols] = joined.astype(BF16)

    for n, b in enumerate(up_blocks):
        if first:
            wait(got_up[n])
        cols = pl.ds(b, BLOCK)
        r.act[:, cols] = gelu(dot(r.normed[...], r.w_up[:, cols]) + r.b_up[:, cols]).astype(BF16)
    if first:
        wait(got_out)
    targets = [(r.piece_a, r.base_a)]
    if len(pieces) > 1:
        targets.append((r.piece_b, r.base_b))
    for n, b in enumerate(down_blocks):
        cols = pl.ds(b, BLOCK)
        summed = dot(r.att[...], r.w_out[:, cols])
        if first:
            wait(got_down[n])
        r.sums[:, cols] = (summed + dot(r.act[...], r.w_down[:, cols])).astype(BF16)
        start = 0
        for piece, (target, base) in zip(pieces, targets):
            size = len(piece) * DRAFT
            span = pl.ds(start, size)
            writes.append(copies.start(r.sums.at[span, cols], target.at[:, cols]))
            for i in range(len(piece)):
                rows_i = pl.ds(start + i * DRAFT, DRAFT)
                kept = r.h[rows_of[start // DRAFT + i], :, cols].astype(F32) + r.bias[:, cols]
                if add_own:
                    kept = kept + r.sums[rows_i, cols].astype(F32)
                r.base[rows_i, cols] = kept
            writes.append(copies.start(r.base.at[span, cols], base.at[:, cols]))
            start += size
    wait(*writes)


def call(kernel, ins, outs, scratch, aliases, name):
    names = (*ins, *outs, *scratch)
    operands = []
    for array, space in ins.values():
        operands.append(array if space is pl.ANY else pltpu.with_memory_space_constraint(array, space))
    results = pl.pallas_call(
        functools.partial(kernel, names),
        out_shape=list(outs.values()),
        in_specs=[pl.BlockSpec(memory_space=space) for _, space in ins.values()],
        out_specs=[pl.BlockSpec(memory_space=ref.memory_space) for ref in outs.values()],
        scratch_shapes=list(scratch.values()),
        input_output_aliases={list(ins).index(a): list(outs).index(b) for a, b in aliases.items()},
        compiler_params=pltpu.CompilerParams(vmem_limit_bytes=VMEM_MIB * 2**20),
        name=name,
    )(*operands)
    return SimpleNamespace(**dict(zip(outs, results)))


def at(space, **arrays):
    return {key: (array, space) for key, array in arrays.items()}


def branch(pieces, a, before):
    requests, _, width = a.hidden.shape
    heads_width = a.qkv_weight.shape[2]
    units = a.up_weight.shape[1]
    cap_len = a.key_cache.shape[1]
    acc_count = a.accepted.shape[1]
    tails = a.split_slot.shape[0]
    count = sum(len(piece) for piece in pieces)
    rows = count * DRAFT
    tail = sum(place >= requests - tails for piece in pieces for place in piece)
    ins = at(
        HBM,
        lengths=a.lengths,
        split_slot=a.split_slot,
        tail_len=a.tail_len,
        accepted=a.accepted,
        parents=a.parents,
        ln_gain=a.ln_gain,
        ln_shift=a.ln_shift,
        qkv_bias=a.qkv_bias,
        up_bias=a.up_bias,
        branch_bias=a.branch_bias,
        hidden=a.hidden,
        key_cache=a.key_cache,
        value_cache=a.value_cache,
    )
    scratch = dict(
        slots=SMEM(a.split_slot.shape, I32),
        own_len=SMEM(a.lengths.shape, I32),
        all_len=SMEM(a.tail_len.shape, I32),
        tree=VMEM(a.parents.shape, I32),
        taken=VMEM(a.accepted.shape, I32),
        gain=VMEM((1, width), F32),
        shift=VMEM((1, width), F32),
        b_qkv=VMEM((3, heads_width), F32),
        b_up=VMEM((1, units), F32),
        bias=VMEM((1, width), F32),
        h=VMEM((count + (0 if tail else tails), DRAFT, width), BF16),
        normed=VMEM((rows, width), BF16),
        k_own=VMEM((count, cap_len, heads_width), BF16),
        v_own=VMEM((count, cap_len, heads_width), BF16),
        q=VMEM((rows, heads_width), BF16),
        k=VMEM((rows, heads_width), BF16),
        v=VMEM((rows, heads_width), BF16),
        att=VMEM((rows, heads_width), BF16),
        act=VMEM((rows, units), BF16),
        sums=VMEM((rows, width), BF16),
        base=VMEM((rows, width), F32),
        picked=VMEM((2, count, acc_count, heads_width), BF16),
        sems=pltpu.SemaphoreType.DMA((100,)),
    )
    outs = dict(rows_out=HBM((2, requests, acc_count, heads_width), BF16))
    aliases = {}
    if before is None:
        ins.update(
            at(
                HBM,
                qkv_weight=a.qkv_weight,
                up_weight=a.up_weight,
                down_weight=a.down_weight,
                out_weight=a.out_weight,
            )
        )
        outs.update(
            w_qkv=VMEM(a.qkv_weight.shape, BF16),
            w_up=VMEM(a.up_weight.shape, BF16),
            w_down=VMEM(a.down_weight.shape, BF16),
            w_out=VMEM(a.out_weight.shape, BF16),
        )
    else:
        ins.update(at(HBM, rows_in=before.rows_out))
        ins.update(at(VMEM, w_qkv=a.w_qkv, w_up=a.w_up, w_down=a.w_down, w_out=a.w_out))
        aliases = dict(rows_in="rows_out")
    if tail:
        ins.update(at(pl.ANY, far_keys=a.far_keys, far_values=a.far_values))
        far_shape = (tail, *a.far_keys.shape[1:])
        scratch.update(k_far=VMEM(far_shape, BF16), v_far=VMEM(far_shape, BF16))
    sizes = [len(piece) * DRAFT for piece in pieces]
    outs.update(piece_a=HBM((sizes[0], width), BF16), base_a=HBM((sizes[0], width), F32))
    if len(sizes) > 1:
        outs.update(piece_b=HBM((sizes[1], width), BF16), base_b=HBM((sizes[1], width), F32))

    def kernel(names, *refs):
        branch_kernel(pieces, before is None, a.n_mp == 2, names, *refs)

    out = call(kernel, ins, outs, scratch, aliases, "branch")
    parts = [(out.piece_a, out.base_a)]
    if len(sizes) > 1:
        parts.append((out.piece_b, out.base_b))
    if before is None:
        a.w_qkv, a.w_up, a.w_down, a.w_out = out.w_qkv, out.w_up, out.w_down, out.w_out
    return parts, out


def finish_kernel(pieces, first, names, *refs):
    r = SimpleNamespace(**{str(name): ref for name, ref in zip(names, refs)})
    given = refs[: len(pieces)]
    kept = refs[len(pieces) : 2 * len(pieces)]
    requests = r.next_qkv.shape[1]
    share = r.new_hidden.shape[0]
    places = [place for piece in pieces for place in piece]
    count = len(places)
    copies = Copies(r.sems)
    got_slots = copies.start(r.split_slot, r.slots)
    got_w = [copies.start(r.next_weight.at[c], r.w_next.at[c]) for c in range(3)] if first else []
    gain = r.next_gain[...]
    shift = r.next_shift[...]
    start = 0
    for n, piece in enumerate(pieces):
        size = len(piece) * DRAFT

        def body(k, carry, n=n, start=start):
            part = pl.ds(pl.multiple_of(k * STEP, STEP), STEP)
            rows = pl.ds(pl.multiple_of(start + k * STEP, STEP), STEP)
            new = (kept[n][part, :] + given[n][part, :].astype(F32)).astype(BF16)
            r.h[rows, :] = new
            r.normed[rows, :] = layer_norm(new.astype(F32), gain, shift).astype(BF16)
            return carry

        lax.fori_loop(0, size // STEP, body, 0, unroll=4)
        start += size

    wait(got_slots)
    order = [request_at(place, r.slots, requests) for place in places]
    rank = lax.axis_index("mp")
    new_writes = []
    for i in range(count):
        copy = copies.make(r.h.at[pl.ds(i * DRAFT, DRAFT)], r.new_hidden.at[order[i] % share])
        owned = order[i] // share == rank
        new_writes.append((owned, copy))
        pl.when(owned)(copy.start)
    writes = []
    for c in range(3):
        wait(*got_w[c : c + 1])
        linear = (dot(r.normed[...], r.w_next[c]) + r.next_bias[pl.ds(c, 1), :]).astype(BF16)
        for i in range(count):
            r.o[c, i] = linear[i * DRAFT : (i + 1) * DRAFT]
            writes.append(copies.start(r.o.at[c, i], r.next_qkv.at[c, order[i]]))
    wait(*writes)
    for owned, copy in new_writes:
        pl.when(owned)(copy.wait)


def finish(sent, a, last):
    requests, _, width = a.hidden.shape
    heads_width = a.next_weight.shape[2]
    share = requests // a.n_mp
    pieces = [piece for piece, _, _ in sent]
    count = sum(len(piece) for piece in pieces)
    rows = count * DRAFT
    ins = {}
    for _, given, _ in sent:
        ins[len(ins)] = (given, VMEM)
    for _, _, base in sent:
        ins[len(ins)] = (base, VMEM)
    ins.update(at(HBM, split_slot=a.split_slot))
    ins.update(at(VMEM, next_gain=a.next_gain, next_shift=a.next_shift, next_bias=a.next_bias))
    aliases = {}
    kept = {}
    if last is None:
        ins.update(at(HBM, next_weight=a.next_weight))
        kept = dict(w_next=VMEM(a.next_weight.shape, BF16))
    else:
        ins.update(at(VMEM, w_next=a.w_next))
        ins.update(at(HBM, new_in=last.new_hidden, qkv_in=last.next_qkv))
        aliases = dict(new_in="new_hidden", qkv_in="next_qkv")
    outs = dict(
        new_hidden=HBM((share, DRAFT, width), BF16),
        next_qkv=HBM((3, requests, DRAFT, heads_width), BF16),
        **kept,
    )
    scratch = dict(
        slots=SMEM(a.split_slot.shape, I32),
        h=VMEM((rows, width), BF16),
        normed=VMEM((rows, width), BF16),
        o=VMEM((3, count, DRAFT, heads_width), BF16),
        sems=pltpu.SemaphoreType.DMA((60,)),
    )

    def kernel(names, *refs):
        finish_kernel(pieces, last is None, names, *refs)

    out = call(kernel, ins, outs, scratch, aliases, "finish")
    if last is None:
        a.w_next = out.w_next
    return out


def local(
    hidden,
    ln_gain,
    ln_shift,
    qkv_weight,
    qkv_bias,
    out_weight,
    up_weight,
    up_bias,
    down_weight,
    branch_bias,
    next_gain,
    next_shift,
    next_weight,
    next_bias,
    key_cache,
    value_cache,
    tail_keys,
    tail_values,
    lengths,
    split_slot,
    tail_len,
    parents,
    accepted,
):
    requests = lengths.shape[0]
    width = hidden.shape[1]
    n_mp = lax.axis_size("mp")
    groups = lax.axis_size("group")
    a = SimpleNamespace(
        hidden=hidden.reshape(requests, DRAFT, width),
        ln_gain=ln_gain.reshape(1, width),
        ln_shift=ln_shift.reshape(1, width),
        qkv_weight=qkv_weight,
        qkv_bias=qkv_bias,
        out_weight=out_weight,
        up_weight=up_weight,
        up_bias=up_bias.reshape(1, -1),
        down_weight=down_weight,
        branch_bias=branch_bias.reshape(1, width),
        next_gain=next_gain.reshape(1, width),
        next_shift=next_shift.reshape(1, width),
        next_weight=next_weight,
        next_bias=next_bias,
        key_cache=key_cache,
        value_cache=value_cache,
        lengths=lengths,
        split_slot=split_slot,
        tail_len=tail_len,
        parents=parents.reshape(requests * DRAFT // PAIR, PAIR),
        accepted=accepted,
        n_mp=n_mp,
    )
    out = None
    sent = []
    for k, pieces in enumerate(CHUNKS):
        if k == 1:
            tail_keys, tail_values, _ = lax.optimization_barrier((tail_keys, tail_values, sent[0][2]))
            swap = [(i, i ^ 1) for i in range(groups)]
            a.far_keys, a.far_values = lax.ppermute((tail_keys, tail_values), "group", swap)
        if k == 2:
            a.lengths, _ = lax.optimization_barrier((a.lengths, sent[k - 2][1]))
        sums, out = branch(pieces, a, out)
        for piece, (part, kept) in zip(pieces, sums):
            if n_mp == 2:
                sent.append((piece, lax.ppermute(part, "mp", [(0, 1), (1, 0)]), kept))
            else:
                sent.append((piece, lax.psum(part, "mp"), kept))
    last = None
    for first, end in FINISHES:
        last = finish(sent[first:end], a, last)
    heads_width = qkv_weight.shape[2]
    return (
        last.new_hidden.reshape(-1, width),
        last.next_qkv.reshape(3, requests * DRAFT, heads_width),
        out.rows_out.reshape(2, -1, heads_width),
    )


def solution(mesh):
    in_specs = (
        P("group", None),
        P(),
        P(),
        P(None, None, "mp"),
        P(None, "mp"),
        P("mp", None),
        P(None, "mp"),
        P("mp"),
        P("mp", None),
        P(),
        P(),
        P(),
        P(None, None, "mp"),
        P(None, "mp"),
        P("group", None, "mp"),
        P("group", None, "mp"),
        P("group", None, "mp"),
        P("group", None, "mp"),
        P("group"),
        P("group"),
        P(),
        P("group"),
        P("group", None),
    )
    out_specs = (P(("group", "mp"), None), P(None, "group", "mp"), P(None, "group", "mp"))
    return jax.shard_map(local, mesh=mesh, in_specs=in_specs, out_specs=out_specs, check_vma=False)
```
